32 devices in a mesh: tm: 8 (over y, x, core), space: 4 (over z).
Axes of the slice: x: 2, y: 2, z: 4, core: 2. Of those that a mesh axis runs over, the one named last changes fastest.
Arguments:
- evecs: bfloat16 [8, 2, 3, 1024, 128], P('tm', None, None, 'space'), may hold values from -2 to 2
- peramb: bfloat16 [8, 4, 8, 2, 128, 128], P('tm', 'space'), may hold values from -0.0234375 to 0.0234375
- momenta: int32 [4, 3], replicated, may hold values from -2 to 2, as said below
- unit_table: int32 [4, 2], replicated, may hold values from 0 to 3, as said below
- time_labels: int32 [8], replicated, may hold values from 0 to 7, each once
Outputs:
- blocks: bfloat16 [8, 4, 8, 2, 128, 128], P('tm', 'space')
The draws below stay inside these ranges and needn't reach their ends.
Inputs may be any that keep to these rules, and one draw needn't show every extreme that they name: `momenta`: the first component of every momentum is one of 1, 2, -1, -2, and each of these four occurs; the other components take any value in range. `unit_table`: column 0 is a permutation of 0 to 3; column 1 lies in 0 to 3 and takes each of these values. `time_labels`: A permutation of 0 to 7.
All inputs are finite; a program needn't handle non-finite values.
Results may differ from the reference program's by a relative error of at most 0.0075.
Values may be sent and summed in bfloat16 or wider, within the bound.
No kernel may reach another device: no remote copies, remote signals or barrier semaphores. Data moves between devices by JAX's collectives and lax.ppermute only.
A program may use at most 64 MiB of HBM per device.

```python
import math
import jax
import jax.numpy as jnp
from jax import lax

LS = 40
NEV = 128
SITES = 1024
NT = 8
NMOM = 4
UNITS = 4


def draw_momenta(key, part):
    key_order = jax.random.fold_in(key, 11)
    key_other = jax.random.fold_in(key, 12)
    order = jax.random.permutation(key_order, NMOM)
    first_values = jnp.array([1, 2, -1, -2], dtype=jnp.int32)
    first_comp = first_values[order % 4]
    others = jax.random.randint(key_other, (NMOM, 2), -2, 3, dtype=jnp.int32)
    return jnp.concatenate([first_comp[:, None], others], axis=1).astype(jnp.int32)


def draw_unit_table(key, part):
    key_moment = jax.random.fold_in(key, 21)
    key_phase = jax.random.fold_in(key, 22)
    moment_order = jax.random.permutation(key_moment, UNITS).astype(jnp.int32)
    phase_order = (jax.random.permutation(key_phase, UNITS) % 4).astype(jnp.int32)
    return jnp.stack([moment_order, phase_order], axis=1)


def shard_levels(stream_key, dims, cuts, low, largest):
    factor_of, own = 1.0, jax.random.fold_in(stream_key, 6)
    for axis_at, parts in cuts:
        draws = jnp.exp(jax.random.uniform(jax.random.fold_in(own, axis_at), (parts,), jnp.float32, low / len(cuts), largest / len(cuts)))
        factor_of = factor_of * jnp.repeat(draws, dims[axis_at] // parts).reshape([-1 if axis == axis_at else 1 for axis in range(len(dims))])
    return factor_of


def centred(own_key, extent, scale, limit, cuts=(), held_as=jnp.bfloat16):
    entries = scale * jax.random.normal(own_key, extent, jnp.float32)
    if cuts:
        entries = entries * shard_levels(own_key, extent, cuts, -0.22, 0.18)
    return jnp.clip(entries, -limit, limit).astype(held_as)


def setup_inputs(seed: int = 0) -> dict:
    streams_of = jax.random.split(jax.random.key(seed), 6)
    evecs = centred(streams_of[0], (NT, 2, 3, SITES, NEV), ((3 * SITES) ** -0.25), 2.0, ((0, 8), (3, 4)))
    peramb = centred(streams_of[1], (NT, UNITS, NT, 2, NEV, NEV), (4 * NEV * NEV) ** -0.5, 0.0234375, ((0, 8), (1, 4)))
    momenta = draw_momenta(jax.random.fold_in(streams_of[5], 71), 0)
    unit_table = draw_unit_table(jax.random.fold_in(streams_of[5], 71), 0)
    time_labels = jax.random.permutation(streams_of[4], NT).astype(jnp.int32)
    return dict(evecs=evecs, peramb=peramb, momenta=momenta, unit_table=unit_table, time_labels=time_labels)


def phase_tables(momenta, first_site, site_count):
    sites = first_site + jnp.arange(site_count, dtype=jnp.int32)
    coords = jnp.stack([sites % LS, (sites // LS) % LS, sites // (LS * LS)], axis=0)
    products = jnp.sum(momenta[:, :, None] * coords[None, :, :], axis=1)
    angles = (products % LS).astype(jnp.float32) * (2.0 * math.pi / LS)
    return jnp.cos(angles), jnp.sin(angles)


def gram(vectors, cosine, sine):
    real_part = vectors[0]
    imag_part = vectors[1]
    cos_site = cosine[None, :, None]
    sin_site = sine[None, :, None]
    phased_real = (cos_site * real_part + sin_site * imag_part).astype(jnp.bfloat16)
    phased_imag = (cos_site * imag_part - sin_site * real_part).astype(jnp.bfloat16)
    columns = vectors.shape[-1]
    left = vectors.reshape(-1, columns)
    right_real = jnp.concatenate([phased_real, phased_imag], axis=0).reshape(-1, columns)
    right_imag = jnp.concatenate([phased_imag, -phased_real], axis=0).reshape(-1, columns)
    gram_real = jnp.dot(left.T, right_real, preferred_element_type=jnp.float32)
    gram_imag = jnp.dot(left.T, right_imag, preferred_element_type=jnp.float32)
    return jnp.stack([gram_real, gram_imag], axis=0)


def chain(sink_block, peramb_rows, sources, time_signs, phase_real, phase_imag):
    left_real = sink_block[0].astype(jnp.float32)
    left_imag = sink_block[1].astype(jnp.float32)
    prop_real = peramb_rows[:, 0].astype(jnp.float32)
    prop_imag = peramb_rows[:, 1].astype(jnp.float32)
    mixed_real = jnp.einsum("ij,njk->nik", left_real, prop_real) - jnp.einsum("ij,njk->nik", left_imag, prop_imag)
    mixed_imag = jnp.einsum("ij,njk->nik", left_real, prop_imag) + jnp.einsum("ij,njk->nik", left_imag, prop_real)
    mixed_real = lax.optimization_barrier(mixed_real.astype(jnp.bfloat16)).astype(jnp.float32)
    mixed_imag = lax.optimization_barrier(mixed_imag.astype(jnp.bfloat16)).astype(jnp.float32)
    source_real = sources[:, 0].astype(jnp.float32)
    source_imag = sources[:, 1].astype(jnp.float32)
    block_real = jnp.einsum("nij,nkj->nik", mixed_real, source_real) + jnp.einsum("nij,nkj->nik", mixed_imag, source_imag)
    block_imag = jnp.einsum("nij,nkj->nik", mixed_imag, source_real) - jnp.einsum("nij,nkj->nik", mixed_real, source_imag)
    scaling = time_signs[:, None, None]
    out_real = scaling * (phase_real * block_real - phase_imag * block_imag)
    out_imag = scaling * (phase_real * block_imag + phase_imag * block_real)
    return jnp.stack([out_real, out_imag], axis=1).astype(jnp.bfloat16)


def reference(evecs, peramb, momenta, unit_table, time_labels):
    cosines, sines = phase_tables(momenta, 0, SITES)

    def per_time(vectors):
        return lax.map(lambda angles: gram(vectors, angles[0], angles[1]), (cosines, sines))

    elementals = lax.map(per_time, evecs).astype(jnp.bfloat16)
    turns = unit_table[:, 1]
    phase_real = ((1 - turns % 2) * (1 - turns)).astype(jnp.float32)
    phase_imag = ((turns % 2) * (2 - turns)).astype(jnp.float32)

    def per_sink(slot):
        sink_label = time_labels[slot]
        time_signs = jnp.where(time_labels > sink_label, -1.0, 1.0).astype(jnp.float32)

        def per_unit(unit):
            moment_index = unit_table[unit, 0]
            sources = jnp.take(elementals, moment_index, axis=1)
            sink_block = sources[slot]
            return chain(sink_block, peramb[slot, unit], sources, time_signs, phase_real[unit], phase_imag[unit])

        return lax.map(per_unit, jnp.arange(UNITS, dtype=jnp.int32))

    return lax.map(per_sink, jnp.arange(NT, dtype=jnp.int32))
```

```python
import functools
import math

import jax
import jax.numpy as jnp
import numpy as np
from jax import lax
from jax.experimental import pallas as pl
from jax.experimental.pallas import tpu as pltpu
from jax.sharding import PartitionSpec as P

LS = 40
LIMIT = 12 * 1024 * 1024
VMEM = pl.BlockSpec(memory_space=pltpu.VMEM)
HBM = pl.BlockSpec(memory_space=pltpu.HBM)


def floor_parts(values, base):
    quotient = jnp.floor((values + 0.5) * (1.0 / base))
    return quotient, values - base * quotient


def gram_kernel(count, evecs, momenta, table, trig, *rest):
    outs = rest[:count]
    vecs, left, moments, units, sems = rest[count:]
    load = pltpu.make_async_copy(evecs, vecs, sems.at[0])
    load_moments = pltpu.make_async_copy(momenta, moments, sems.at[1])
    load_units = pltpu.make_async_copy(table, units, sems.at[2])
    load.start()
    load_moments.start()
    load_units.start()
    me = lax.axis_index("space")
    colours, sites, columns = vecs.shape[1:]
    first = (me * sites).astype(jnp.float32)
    site = lax.broadcasted_iota(jnp.int32, (sites, columns), 0).astype(jnp.float32) + first
    row, x = floor_parts(site, float(LS))
    z, y = floor_parts(row, float(LS))
    load_moments.wait()
    load_units.wait()
    load.wait()
    for part in range(2):
        for colour in range(colours):
            left[pl.ds(part * columns, columns), pl.ds(colour * sites, sites)] = vecs[part, colour].T
    cos_table = jnp.broadcast_to(trig[0:1, :], (sites, columns))
    sin_table = jnp.broadcast_to(trig[1:2, :], (sites, columns))
    for k in range(count):
        moment = units[0, me ^ k]
        px = moments[moment, 0].astype(jnp.float32)
        py = moments[moment, 1].astype(jnp.float32)
        pz = moments[moment, 2].astype(jnp.float32)
        _, turns = floor_parts(px * x + py * y + pz * z, float(LS))
        index = turns.astype(jnp.int32)
        cosine = jnp.take_along_axis(cos_table, index, axis=1)
        sine = jnp.take_along_axis(sin_table, index, axis=1)
        total = None
        for colour in range(colours):
            real = vecs[0, colour].astype(jnp.float32)
            imag = vecs[1, colour].astype(jnp.float32)
            phased = jnp.concatenate(
                [
                    (cosine * real + sine * imag).astype(jnp.bfloat16),
                    (cosine * imag - sine * real).astype(jnp.bfloat16),
                ],
                axis=1,
            )
            term = jnp.dot(
                left[:, pl.ds(colour * sites, sites)], phased, preferred_element_type=jnp.float32
            )
            total = term if total is None else total + term
        outs[k][0] = (total[:columns, :columns] + total[columns:, columns:]).astype(outs[k].dtype)
        outs[k][1] = (total[:columns, columns:] - total[columns:, :columns]).astype(outs[k].dtype)


def partial_elementals(vectors, momenta, table, count):
    _, colours, sites, columns = vectors.shape
    angles = np.arange(128, dtype=np.float32) * np.float32(2.0 * math.pi / LS)
    trig = jnp.asarray(np.stack([np.cos(angles), np.sin(angles)] * 4).astype(np.float32))
    shape = (2, columns, columns)
    return pl.pallas_call(
        functools.partial(gram_kernel, count),
        out_shape=[
            jax.ShapeDtypeStruct(shape, jnp.float32 if k == 0 else jnp.bfloat16)
            for k in range(count)
        ],
        in_specs=[HBM, HBM, HBM, VMEM],
        out_specs=[VMEM] * count,
        scratch_shapes=[
            pltpu.VMEM(vectors.shape, vectors.dtype),
            pltpu.VMEM((2 * columns, colours * sites), vectors.dtype),
            pltpu.SMEM(momenta.shape, jnp.int32),
            pltpu.SMEM(table.shape, jnp.int32),
            pltpu.SemaphoreType.DMA((3,)),
        ],
        compiler_params=pltpu.CompilerParams(vmem_limit_bytes=LIMIT),
        cost_estimate=pl.CostEstimate(
            flops=count * 16 * colours * sites * columns * columns,
            bytes_accessed=4 * colours * sites * columns + count * 4 * columns * columns,
            transcendentals=0,
        ),
        name="gram",
    )(vectors, momenta, table, trig)


def mix_kernel(sink, peramb, table, labels, out, units, times, sems):
    load_units = pltpu.make_async_copy(table, units, sems.at[0])
    load_times = pltpu.make_async_copy(labels, times, sems.at[1])
    load_units.start()
    load_times.start()
    real = sink[0]
    imag = sink[1]
    columns = real.shape[0]
    left = jnp.concatenate(
        [jnp.concatenate([real, -imag], axis=1), jnp.concatenate([imag, real], axis=1)], axis=0
    )
    load_units.wait()
    load_times.wait()
    turns = units[1, lax.axis_index("space")]
    odd = lax.rem(turns, 2)
    phase_real = ((1 - odd) * (1 - turns)).astype(jnp.float32)
    phase_imag = (odd * (2 - turns)).astype(jnp.float32)
    own = times[lax.axis_index("tm")]
    for n in range(peramb.shape[0]):
        sign = jnp.where(times[n] > own, -1.0, 1.0).astype(jnp.float32)
        right = jnp.concatenate([peramb[n, 0], peramb[n, 1]], axis=0)
        mixed = jnp.dot(left, right, preferred_element_type=jnp.float32)
        mixed_real = mixed[:columns]
        mixed_imag = mixed[columns:]
        turn_real = sign * phase_real
        turn_imag = sign * phase_imag
        out[n, :, pl.ds(0, columns)] = (turn_real * mixed_real - turn_imag * mixed_imag).astype(
            out.dtype
        )
        out[n, :, pl.ds(columns, columns)] = (
            turn_real * mixed_imag + turn_imag * mixed_real
        ).astype(out.dtype)


def mix(sink, peramb, table, labels):
    slots, _, columns, _ = peramb.shape
    return pl.pallas_call(
        mix_kernel,
        out_shape=jax.ShapeDtypeStruct((slots, columns, 2 * columns), jnp.bfloat16),
        in_specs=[VMEM, VMEM, HBM, HBM],
        out_specs=VMEM,
        scratch_shapes=[
            pltpu.SMEM(table.shape, jnp.int32),
            pltpu.SMEM(labels.shape, jnp.int32),
            pltpu.SemaphoreType.DMA((2,)),
        ],
        compiler_params=pltpu.CompilerParams(vmem_limit_bytes=LIMIT),
        cost_estimate=pl.CostEstimate(
            flops=slots * 8 * columns**3, bytes_accessed=slots * 8 * columns**2, transcendentals=0
        ),
        name="mix",
    )(sink, peramb, table, labels)


def close_kernel(mixed, sources, out):
    columns = sources.shape[-1]
    for n in range(mixed.shape[0]):
        real = sources[n, 0]
        imag = sources[n, 1]
        right = jnp.concatenate(
            [jnp.concatenate([real, imag], axis=1), jnp.concatenate([-imag, real], axis=1)], axis=0
        )
        block = lax.dot_general(
            mixed[n], right, (((1,), (1,)), ((), ())), preferred_element_type=jnp.float32
        )
        out[n, 0] = block[:, :columns].astype(out.dtype)
        out[n, 1] = block[:, columns:].astype(out.dtype)


def close(mixed, sources):
    slots, columns, _ = mixed.shape
    return pl.pallas_call(
        close_kernel,
        out_shape=jax.ShapeDtypeStruct((slots, 2, columns, columns), jnp.bfloat16),
        in_specs=[VMEM, VMEM],
        out_specs=VMEM,
        compiler_params=pltpu.CompilerParams(vmem_limit_bytes=LIMIT),
        cost_estimate=pl.CostEstimate(
            flops=slots * 8 * columns**3, bytes_accessed=slots * 12 * columns**2, transcendentals=0
        ),
        name="close",
    )(mixed, sources)


def swap(value, axis, size, distance):
    return lax.ppermute(value, axis, [(a, a ^ distance) for a in range(size)])


def body(space, evecs, peramb, momenta, unit_table, time_labels):
    table = unit_table.T
    partials = partial_elementals(evecs[0], momenta, table, space)
    total = partials[0]
    arrived = [swap(partials[k], "space", space, k) for k in range(space - 1, 0, -1)]
    for value in arrived:
        total = total + value.astype(jnp.float32)
    sink = total.astype(jnp.bfloat16)
    sources = lax.all_gather(sink[None], "tm", axis=0, tiled=True)
    mixed = mix(sink, peramb[0, 0], table, time_labels)
    return close(mixed, sources)[None, None]


def solution(mesh):
    return jax.shard_map(
        functools.partial(body, mesh.shape["space"]),
        mesh=mesh,
        in_specs=(
            P("tm", None, None, "space", None),
            P("tm", "space", None, None, None, None),
            P(),
            P(),
            P(),
        ),
        out_specs=P("tm", "space", None, None, None, None),
        check_vma=False,
    )
```

```python
import functools
import math

import jax
import jax.numpy as jnp
import numpy as np
from jax import lax
from jax.experimental import pallas as pl
from jax.experimental.pallas import tpu as pltpu
from jax.sharding import PartitionSpec as P


LS = 40
LIMIT = 12 * 1024 * 1024
VMEM = pl.BlockSpec(memory_space=pltpu.VMEM)
HBM = pl.BlockSpec(memory_space=pltpu.HBM)


def floor_parts(values, base):
    quotient = jnp.floor((values + 0.5) * (1.0 / base))
    return quotient, values - base * quotient


def in_hbm(value):
    return pltpu.with_memory_space_constraint(value, pltpu.HBM)


def site_parts(sites, columns):
    first = (lax.axis_index("space") * sites).astype(jnp.float32)
    site = lax.broadcasted_iota(jnp.int32, (sites, columns), 0).astype(jnp.float32) + first
    row, x = floor_parts(site, float(LS))
    z, y = floor_parts(row, float(LS))
    return x, y, z


def gram(vecs, left, moments, units, tables, parts, k):
    _, colours, sites, columns = vecs.shape
    x, y, z = parts
    moment = units[0, lax.axis_index("space") ^ k]
    px = moments[moment, 0].astype(jnp.float32)
    py = moments[moment, 1].astype(jnp.float32)
    pz = moments[moment, 2].astype(jnp.float32)
    _, turns = floor_parts(px * x + py * y + pz * z, float(LS))
    index = turns.astype(jnp.int32)
    cosine = jnp.take_along_axis(tables[0], index, axis=1)
    sine = jnp.take_along_axis(tables[1], index, axis=1)
    total = None
    for colour in range(colours):
        real = vecs[0, colour].astype(jnp.float32)
        imag = vecs[1, colour].astype(jnp.float32)
        phased = jnp.concatenate(
            [
                (cosine * real + sine * imag).astype(jnp.bfloat16),
                (cosine * imag - sine * real).astype(jnp.bfloat16),
            ],
            axis=1,
        )
        term = jnp.dot(
            left[:, pl.ds(colour * sites, sites)], phased, preferred_element_type=jnp.float32
        )
        total = term if total is None else total + term
    real = total[:columns, :columns] + total[columns:, columns:]
    imag = total[:columns, columns:] - total[columns:, :columns]
    return real, imag


def spread(trig, sites, columns):
    return [jnp.broadcast_to(trig[i : i + 1, :], (sites, columns)) for i in range(2)]


def gram_first(ks, evecs, momenta, table, trig_in, *rest):
    outs = rest[: len(ks)]
    vecs, left, trig, moments, units, sems = rest[len(ks) :]
    loads = [
        pltpu.make_async_copy(source, target, sems.at[i])
        for i, (source, target) in enumerate(
            ((evecs, vecs), (momenta, moments), (table, units), (trig_in, trig))
        )
    ]
    for load in loads:
        load.start()
    _, colours, sites, columns = vecs.shape
    parts = site_parts(sites, columns)
    for load in loads[::-1]:
        load.wait()
    for part in range(2):
        for colour in range(colours):
            left[pl.ds(part * columns, columns), pl.ds(colour * sites, sites)] = vecs[part, colour].T
    tables = spread(trig, sites, columns)
    for out, k in zip(outs, ks):
        real, imag = gram(vecs, left, moments, units, tables, parts, k)
        out[0] = real.astype(out.dtype)
        out[1] = imag.astype(out.dtype)


def gram_second(ks, vecs, left, trig, momenta, table, *rest):
    outs = rest[: len(ks)]
    moments, units, sems = rest[len(ks) :]
    loads = [
        pltpu.make_async_copy(source, target, sems.at[i])
        for i, (source, target) in enumerate(((momenta, moments), (table, units)))
    ]
    for load in loads:
        load.start()
    _, _, sites, columns = vecs.shape
    parts = site_parts(sites, columns)
    tables = spread(trig, sites, columns)
    for load in loads:
        load.wait()
    for out, k in zip(outs, ks):
        real, imag = gram(vecs, left, moments, units, tables, parts, k)
        out[0] = real.astype(out.dtype)
        out[1] = imag.astype(out.dtype)


def gram_cost(count, vectors):
    _, colours, sites, columns = vectors.shape
    return pl.CostEstimate(
        flops=count * 16 * colours * sites * columns * columns,
        bytes_accessed=4 * colours * sites * columns + count * 4 * columns * columns,
        transcendentals=0,
    )


def partial_elementals(vectors, momenta, table, count):
    _, colours, sites, columns = vectors.shape
    angles = np.arange(128, dtype=np.float32) * np.float32(2.0 * math.pi / LS)
    trig = jnp.asarray(np.stack([np.cos(angles), np.sin(angles)] * 4).astype(np.float32))
    shape = (2, columns, columns)
    far = list(range(count - 1, count // 2 - 1, -1))
    near = list(range(count // 2 - 1, -1, -1))
    momenta, table = in_hbm(momenta), in_hbm(table)
    small = [pltpu.SMEM(momenta.shape, jnp.int32), pltpu.SMEM(table.shape, jnp.int32)]
    params = pltpu.CompilerParams(vmem_limit_bytes=LIMIT)
    *first, vecs, left, trig = pl.pallas_call(
        functools.partial(gram_first, far),
        out_shape=[jax.ShapeDtypeStruct(shape, jnp.bfloat16) for _ in far]
        + [
            jax.ShapeDtypeStruct(vectors.shape, vectors.dtype),
            jax.ShapeDtypeStruct((2 * columns, colours * sites), vectors.dtype),
            jax.ShapeDtypeStruct(trig.shape, trig.dtype),
        ],
        in_specs=[HBM] * 4,
        out_specs=[VMEM] * (len(far) + 3),
        scratch_shapes=small + [pltpu.SemaphoreType.DMA((4,))],
        compiler_params=params,
        cost_estimate=gram_cost(len(far), vectors),
        name="gram_far",
    )(in_hbm(vectors), momenta, table, in_hbm(trig))
    second = pl.pallas_call(
        functools.partial(gram_second, near),
        out_shape=[
            jax.ShapeDtypeStruct(shape, jnp.float32 if k == 0 else jnp.bfloat16) for k in near
        ],
        in_specs=[VMEM] * 3 + [HBM] * 2,
        out_specs=[VMEM] * len(near),
        scratch_shapes=small + [pltpu.SemaphoreType.DMA((2,))],
        compiler_params=params,
        cost_estimate=gram_cost(len(near), vectors),
        name="gram_near",
    )(vecs, left, trig, momenta, table)
    return dict(zip(far + near, first + list(second)))


def mix_kernel(sink, peramb, table, labels, out, units, times, sems):
    load_units = pltpu.make_async_copy(table, units, sems.at[0])
    load_times = pltpu.make_async_copy(labels, times, sems.at[1])
    load_units.start()
    load_times.start()
    real = sink[0]
    imag = sink[1]
    columns = real.shape[0]
    left = jnp.concatenate(
        [jnp.concatenate([real, -imag], axis=1), jnp.concatenate([imag, real], axis=1)], axis=0
    )
    load_units.wait()
    load_times.wait()
    turns = units[1, lax.axis_index("space")]
    odd = lax.rem(turns, 2)
    phase_real = ((1 - odd) * (1 - turns)).astype(jnp.float32)
    phase_imag = (odd * (2 - turns)).astype(jnp.float32)
    me = lax.axis_index("tm")
    own = times[me]
    for k in range(peramb.shape[0]):
        n = me ^ k
        sign = jnp.where(times[n] > own, -1.0, 1.0).astype(jnp.float32)
        right = jnp.concatenate([peramb[n, 0], peramb[n, 1]], axis=0)
        mixed = jnp.dot(left, right, preferred_element_type=jnp.float32)
        mixed_real = mixed[:columns]
        mixed_imag = mixed[columns:]
        turn_real = sign * phase_real
        turn_imag = sign * phase_imag
        out[k, :, pl.ds(0, columns)] = (turn_real * mixed_real - turn_imag * mixed_imag).astype(
            out.dtype
        )
        out[k, :, pl.ds(columns, columns)] = (
            turn_real * mixed_imag + turn_imag * mixed_real
        ).astype(out.dtype)


def mix(sink, peramb, table, labels):
    slots, _, columns, _ = peramb.shape
    return pl.pallas_call(
        mix_kernel,
        out_shape=jax.ShapeDtypeStruct((slots, columns, 2 * columns), jnp.bfloat16),
        in_specs=[VMEM, VMEM, HBM, HBM],
        out_specs=VMEM,
        scratch_shapes=[
            pltpu.SMEM(table.shape, jnp.int32),
            pltpu.SMEM(labels.shape, jnp.int32),
            pltpu.SemaphoreType.DMA((2,)),
        ],
        compiler_params=pltpu.CompilerParams(vmem_limit_bytes=LIMIT),
        cost_estimate=pl.CostEstimate(
            flops=slots * 8 * columns**3, bytes_accessed=slots * 8 * columns**2, transcendentals=0
        ),
        name="mix",
    )(sink, peramb, in_hbm(table), in_hbm(labels))


def close_kernel(ks, before, mixed, *rest):
    sources = rest[: len(ks)]
    out, blocks, sems = rest[len(ks) + before :]
    columns = sources[0].shape[-1]
    me = lax.axis_index("tm")
    stores = []
    for i, (source, k) in enumerate(zip(sources, ks)):
        real = source[0]
        imag = source[1]
        right = jnp.concatenate(
            [jnp.concatenate([real, imag], axis=1), jnp.concatenate([-imag, real], axis=1)], axis=0
        )
        block = lax.dot_general(
            mixed[k], right, (((1,), (1,)), ((), ())), preferred_element_type=jnp.float32
        )
        blocks[i, 0] = block[:, :columns].astype(out.dtype)
        blocks[i, 1] = block[:, columns:].astype(out.dtype)
        store = pltpu.make_async_copy(blocks.at[i], out.at[me ^ k], sems.at[i])
        store.start()
        stores.append(store)
    for store in stores:
        store.wait()


def close(mixed, sources, ks, out=None):
    slots, columns, _ = mixed.shape
    before = [] if out is None else [out]
    shape = (slots, 2, columns, columns)
    return pl.pallas_call(
        functools.partial(close_kernel, ks, len(before)),
        out_shape=jax.ShapeDtypeStruct(shape, jnp.bfloat16),
        in_specs=[VMEM] * (1 + len(ks)) + [HBM] * len(before),
        out_specs=HBM,
        scratch_shapes=[
            pltpu.VMEM((len(ks),) + shape[1:], jnp.bfloat16),
            pltpu.SemaphoreType.DMA((len(ks),)),
        ],
        input_output_aliases={1 + len(ks): 0} if before else {},
        compiler_params=pltpu.CompilerParams(vmem_limit_bytes=LIMIT),
        cost_estimate=pl.CostEstimate(
            flops=len(ks) * 8 * columns**3,
            bytes_accessed=len(ks) * 12 * columns**2,
            transcendentals=0,
        ),
        name="close",
    )(mixed, *[sources[k] for k in ks], *before)


def swap(value, axis, size, distance):
    return lax.ppermute(value, axis, [(a, a ^ distance) for a in range(size)])


def body(space, times, evecs, peramb, momenta, unit_table, time_labels):
    table = unit_table.T
    partials = partial_elementals(evecs[0], momenta, table, space)
    total = partials[0]
    for k in range(1, space):
        total = total + swap(partials[k], "space", space, k).astype(jnp.float32)
    sink = total.astype(jnp.bfloat16)
    sources = {0: sink}
    for k in range(2, times, 2):
        sources[k] = swap(sink, "tm", times, k)
    mixed = mix(sink, peramb[0, 0], table, time_labels)
    for k in range(0, times, 2):
        sources[k + 1] = swap(sources[k], "tm", times, 1)
    last = [times - 2, times - 1]
    out = close(mixed, sources, [k for k in range(times) if k not in last])
    return close(mixed, sources, last, out)[None, None]


def solution(mesh):
    space, times = mesh.shape["space"], mesh.shape["tm"]
    return jax.shard_map(
        functools.partial(body, space, times),
        mesh=mesh,
        in_specs=(
            P("tm", None, None, "space", None),
            P("tm", "space", None, None, None, None),
            P(),
            P(),
            P(),
        ),
        out_specs=P("tm", "space", None, None, None, None),
        check_vma=False,
    )
```

```python
import functools
import math

import jax
import jax.numpy as jnp
import numpy as np
from jax import lax
from jax.experimental import pallas as pl
from jax.experimental.pallas import tpu as pltpu
from jax.sharding import PartitionSpec as P


LS = 40
LIMIT = 12 * 1024 * 1024
VMEM = pl.BlockSpec(memory_space=pltpu.VMEM)
HBM = pl.BlockSpec(memory_space=pltpu.HBM)


def floor_parts(values, base):
    quotient = jnp.floor((values + 0.5) * (1.0 / base))
    return quotient, values - base * quotient


def in_hbm(value):
    return pltpu.with_memory_space_constraint(value, pltpu.HBM)


def site_parts(sites, columns):
    first = (lax.axis_index("space") * sites).astype(jnp.float32)
    site = lax.broadcasted_iota(jnp.int32, (sites, columns), 0).astype(jnp.float32) + first
    row, x = floor_parts(site, float(LS))
    z, y = floor_parts(row, float(LS))
    return x, y, z


def momentum(moments, units, shift):
    unit = lax.rem(lax.axis_index("space") + shift, lax.axis_size("space"))
    moment = units[0, unit]
    return [moments[moment, i].astype(jnp.float32) for i in range(3)]


def gram(vecs, left, tables, parts, factors):
    _, colours, sites, columns = vecs.shape
    x, y, z = parts
    px, py, pz = factors
    _, turns = floor_parts(px * x + py * y + pz * z, float(LS))
    index = turns.astype(jnp.int32)
    cosine = jnp.take_along_axis(tables[0], index, axis=1)
    sine = jnp.take_along_axis(tables[1], index, axis=1)
    total = None
    for colour in range(colours):
        real = vecs[0, colour].astype(jnp.float32)
        imag = vecs[1, colour].astype(jnp.float32)
        phased = jnp.concatenate(
            [
                (cosine * real + sine * imag).astype(jnp.bfloat16),
                (cosine * imag - sine * real).astype(jnp.bfloat16),
            ],
            axis=1,
        )
        term = jnp.dot(
            left[:, pl.ds(colour * sites, sites)], phased, preferred_element_type=jnp.float32
        )
        total = term if total is None else total + term
    real = total[:columns, :columns] + total[columns:, columns:]
    imag = total[:columns, columns:] - total[columns:, :columns]
    return real, imag


def spread(trig, sites, columns):
    return [jnp.broadcast_to(trig[i : i + 1, :], (sites, columns)) for i in range(2)]


def gram_first(far, near, evecs, momenta, table, trig_in, *rest):
    outs = rest[: len(far)]
    vecs, left, trig, factors, moments, units, sems = rest[len(far) :]
    loads = [
        pltpu.make_async_copy(source, target, sems.at[i])
        for i, (source, target) in enumerate(
            ((evecs, vecs), (momenta, moments), (table, units), (trig_in, trig))
        )
    ]
    for load in loads:
        load.start()
    _, colours, sites, columns = vecs.shape
    parts = site_parts(sites, columns)
    for load in loads[::-1]:
        load.wait()
    for part in range(2):
        for colour in range(colours):
            left[pl.ds(part * columns, columns), pl.ds(colour * sites, sites)] = vecs[part, colour].T
    tables = spread(trig, sites, columns)
    for i, k in enumerate(near):
        for j, factor in enumerate(momentum(moments, units, k)):
            factors[i, j] = jnp.full(factors.shape[2:], factor, jnp.float32)
    for out, k in zip(outs, far):
        real, imag = gram(vecs, left, tables, parts, momentum(moments, units, k))
        out[0] = real.astype(out.dtype)
        out[1] = imag.astype(out.dtype)


def gram_second(vecs, left, trig, factors, *outs):
    _, _, sites, columns = vecs.shape
    parts = site_parts(sites, columns)
    tables = spread(trig, sites, columns)
    for i, out in enumerate(outs):
        own = [jnp.broadcast_to(factors[i, j, 0:1], (sites, columns)) for j in range(3)]
        real, imag = gram(vecs, left, tables, parts, own)
        out[0] = real.astype(out.dtype)
        out[1] = imag.astype(out.dtype)


def gram_cost(count, vectors):
    _, colours, sites, columns = vectors.shape
    return pl.CostEstimate(
        flops=count * 16 * colours * sites * columns * columns,
        bytes_accessed=4 * colours * sites * columns + count * 4 * columns * columns,
        transcendentals=0,
    )


def partial_elementals(vectors, momenta, table, far, near):
    _, colours, sites, columns = vectors.shape
    angles = np.arange(128, dtype=np.float32) * np.float32(2.0 * math.pi / LS)
    trig = jnp.asarray(np.stack([np.cos(angles), np.sin(angles)] * 4).astype(np.float32))
    shape = (2, columns, columns)
    momenta, table = in_hbm(momenta), in_hbm(table)
    small = [pltpu.SMEM(momenta.shape, jnp.int32), pltpu.SMEM(table.shape, jnp.int32)]
    params = pltpu.CompilerParams(vmem_limit_bytes=LIMIT)
    *first, vecs, left, trig, factors = pl.pallas_call(
        functools.partial(gram_first, far, near),
        out_shape=[jax.ShapeDtypeStruct(shape, jnp.bfloat16) for _ in far]
        + [
            jax.ShapeDtypeStruct(vectors.shape, vectors.dtype),
            jax.ShapeDtypeStruct((2 * columns, colours * sites), vectors.dtype),
            jax.ShapeDtypeStruct(trig.shape, trig.dtype),
            jax.ShapeDtypeStruct((len(near), 3, 8, columns), jnp.float32),
        ],
        in_specs=[HBM] * 4,
        out_specs=[VMEM] * (len(far) + 4),
        scratch_shapes=small + [pltpu.SemaphoreType.DMA((4,))],
        compiler_params=params,
        cost_estimate=gram_cost(len(far), vectors),
        name="gram_far",
    )(in_hbm(vectors), momenta, table, in_hbm(trig))
    second = pl.pallas_call(
        gram_second,
        out_shape=[
            jax.ShapeDtypeStruct(shape, jnp.float32 if k == 0 else jnp.bfloat16) for k in near
        ],
        in_specs=[VMEM] * 4,
        out_specs=[VMEM] * len(near),
        compiler_params=params,
        cost_estimate=gram_cost(len(near), vectors),
        name="gram_near",
    )(vecs, left, trig, factors)
    return dict(zip(far + near, first + list(second)))


def mix_kernel(sink, peramb, table, labels, out, units, times, sems):
    load_units = pltpu.make_async_copy(table, units, sems.at[0])
    load_times = pltpu.make_async_copy(labels, times, sems.at[1])
    load_units.start()
    load_times.start()
    real = sink[0]
    imag = sink[1]
    columns = real.shape[0]
    left = jnp.concatenate(
        [jnp.concatenate([real, -imag], axis=1), jnp.concatenate([imag, real], axis=1)], axis=0
    )
    load_units.wait()
    load_times.wait()
    turns = units[1, lax.axis_index("space")]
    odd = lax.rem(turns, 2)
    phase_real = ((1 - odd) * (1 - turns)).astype(jnp.float32)
    phase_imag = (odd * (2 - turns)).astype(jnp.float32)
    me = lax.axis_index("tm")
    own = times[me]
    for k in range(peramb.shape[0]):
        n = lax.axis_index("tm") ^ k
        sign = jnp.where(times[n] > own, -1.0, 1.0).astype(jnp.float32)
        right = jnp.concatenate([peramb[n, 0], peramb[n, 1]], axis=0)
        mixed = jnp.dot(left, right, preferred_element_type=jnp.float32)
        mixed_real = mixed[:columns]
        mixed_imag = mixed[columns:]
        turn_real = sign * phase_real
        turn_imag = sign * phase_imag
        out[k, :, pl.ds(0, columns)] = (turn_real * mixed_real - turn_imag * mixed_imag).astype(
            out.dtype
        )
        out[k, :, pl.ds(columns, columns)] = (
            turn_real * mixed_imag + turn_imag * mixed_real
        ).astype(out.dtype)


def mix(sink, peramb, table, labels):
    slots, _, columns, _ = peramb.shape
    return pl.pallas_call(
        mix_kernel,
        out_shape=jax.ShapeDtypeStruct((slots, columns, 2 * columns), jnp.bfloat16),
        in_specs=[VMEM, VMEM, HBM, HBM],
        out_specs=VMEM,
        scratch_shapes=[
            pltpu.SMEM(table.shape, jnp.int32),
            pltpu.SMEM(labels.shape, jnp.int32),
            pltpu.SemaphoreType.DMA((2,)),
        ],
        compiler_params=pltpu.CompilerParams(vmem_limit_bytes=LIMIT),
        cost_estimate=pl.CostEstimate(
            flops=slots * 8 * columns**3, bytes_accessed=slots * 8 * columns**2, transcendentals=0
        ),
        name="mix",
    )(sink, peramb, in_hbm(table), in_hbm(labels))


def close_kernel(ks, before, mixed, *rest):
    sources = rest[: len(ks)]
    out, blocks, sems = rest[len(ks) + before :]
    columns = sources[0].shape[-1]
    stores = []
    for i, (source, k) in enumerate(zip(sources, ks)):
        real = source[0]
        imag = source[1]
        right = jnp.concatenate(
            [jnp.concatenate([real, imag], axis=1), jnp.concatenate([-imag, real], axis=1)], axis=0
        )
        block = lax.dot_general(
            mixed[k], right, (((1,), (1,)), ((), ())), preferred_element_type=jnp.float32
        )
        blocks[i, 0] = block[:, :columns].astype(out.dtype)
        blocks[i, 1] = block[:, columns:].astype(out.dtype)
        store = pltpu.make_async_copy(blocks.at[i], out.at[lax.axis_index("tm") ^ k], sems.at[i])
        store.start()
        stores.append(store)
    for store in stores:
        store.wait()


def close(mixed, sources, ks, out=None):
    slots, columns, _ = mixed.shape
    before = [] if out is None else [out]
    shape = (slots, 2, columns, columns)
    return pl.pallas_call(
        functools.partial(close_kernel, ks, len(before)),
        out_shape=jax.ShapeDtypeStruct(shape, jnp.bfloat16),
        in_specs=[VMEM] * (1 + len(ks)) + [HBM] * len(before),
        out_specs=HBM,
        scratch_shapes=[
            pltpu.VMEM((len(ks),) + shape[1:], jnp.bfloat16),
            pltpu.SemaphoreType.DMA((len(ks),)),
        ],
        input_output_aliases={1 + len(ks): 0} if before else {},
        compiler_params=pltpu.CompilerParams(vmem_limit_bytes=LIMIT),
        cost_estimate=pl.CostEstimate(
            flops=len(ks) * 8 * columns**3,
            bytes_accessed=len(ks) * 12 * columns**2,
            transcendentals=0,
        ),
        name="close",
    )(mixed, *[sources[k] for k in ks], *before)


def sum_order(space):
    shifts = list(range(1, space))
    far = space // 2
    return shifts, far


def hop_order(times):
    return [times - 2] + list(range(2, times - 2, 2))


def body(space, times, evecs, peramb, momenta, unit_table, time_labels):
    table = unit_table.T
    shifts, far = sum_order(space)
    partials = partial_elementals(evecs[0], momenta, table, shifts[:far], shifts[far:] + [0])
    total = partials[0]
    for shift in shifts:
        pairs = [(a, (a + shift) % space) for a in range(space)]
        total = total + lax.ppermute(partials[shift], "space", pairs).astype(jnp.float32)
    sink = total.astype(jnp.bfloat16)
    sources = {0: sink}
    hops = hop_order(times)
    for k in hops:
        sources[k] = lax.ppermute(sink, "tm", [(a, a ^ k) for a in range(times)])
    mixed = mix(sink, peramb[0, 0], table, time_labels)
    for k in [0] + hops:
        sources[k + 1] = lax.ppermute(sources[k], "tm", [(a, a ^ 1) for a in range(times)])
    last = [k + i for k in hops[-2:] for i in range(2)]
    out = close(mixed, sources, [k for k in range(times) if k not in last])
    return close(mixed, sources, last, out)[None, None]


def solution(mesh):
    space, times = mesh.shape["space"], mesh.shape["tm"]
    return jax.shard_map(
        functools.partial(body, space, times),
        mesh=mesh,
        in_specs=(
            P("tm", None, None, "space", None),
            P("tm", "space", None, None, None, None),
            P(),
            P(),
            P(),
        ),
        out_specs=P("tm", "space", None, None, None, None),
        check_vma=False,
    )
```

```python
import functools
import math

import jax
import jax.numpy as jnp
import numpy as np
from jax import lax
from jax.experimental import pallas as pl
from jax.experimental.pallas import tpu as pltpu
from jax.sharding import PartitionSpec as P


LS = 40
LATE = 4
LIMIT = 12 * 1024 * 1024
VMEM = pl.BlockSpec(memory_space=pltpu.VMEM)
HBM = pl.BlockSpec(memory_space=pltpu.HBM)


def floor_parts(values, base):
    quotient = jnp.floor((values + 0.5) * (1.0 / base))
    return quotient, values - base * quotient


def in_hbm(value):
    return pltpu.with_memory_space_constraint(value, pltpu.HBM)


def site_parts(count, sites):
    first = (lax.axis_index("space") * sites).astype(jnp.float32)
    site = lax.broadcasted_iota(jnp.int32, (count, sites), 1).astype(jnp.float32) + first
    row, x = floor_parts(site, float(LS))
    if sites * lax.axis_size("space") <= LS * LS:
        return [x, row]
    z, y = floor_parts(row, float(LS))
    return [x, y, z]


def ring(size):
    return [at ^ (at >> 1) for at in range(size)]


def partner(size, shift):
    places = ring(size)
    me = lax.axis_index("space")
    target = jnp.int32(0)
    for at, place in enumerate(places):
        target = jnp.where(me == place, places[(at + shift) % size], target)
    return target


def along(size, shift):
    places = ring(size)
    return [(place, places[(at + shift) % size]) for at, place in enumerate(places)]


def phases(moments, units, trig, shifts, sites, targets):
    count = len(shifts)
    which = lax.broadcasted_iota(jnp.int32, (count, sites), 0)
    rows = [
        units[0, partner(lax.axis_size("space"), shift)]
        for shift in shifts
    ]
    product = jnp.zeros((count, sites), jnp.float32)
    for i, part in enumerate(site_parts(count, sites)):
        factor = jnp.zeros((count, sites), jnp.float32)
        for k, row in enumerate(rows):
            factor = jnp.where(which == k, moments[row, i].astype(jnp.float32), factor)
        product = product + factor * part
    _, turns = floor_parts(product, float(LS))
    index = turns.astype(jnp.int32)
    lanes = trig.shape[1]
    values = []
    for i in range(2):
        table = jnp.broadcast_to(trig[i : i + 1, :], (count, lanes))
        pieces = [
            jnp.take_along_axis(
                table, index[:, at : at + lanes], axis=1, mode="promise_in_bounds"
            )
            for at in range(0, sites, lanes)
        ]
        values.append(jnp.concatenate(pieces, axis=1))
    rest = jnp.concatenate(values, axis=0)
    pieces = []
    for _ in range(3):
        piece = rest.astype(jnp.bfloat16).astype(jnp.float32)
        pieces.append(piece)
        rest = rest - piece
    left = jnp.concatenate(pieces, axis=0).astype(jnp.bfloat16)
    shape = (left.shape[0], 2 * count * lanes)
    row = lax.rem(lax.broadcasted_iota(jnp.int32, shape, 0), 2 * count)
    column = lax.div(lax.broadcasted_iota(jnp.int32, shape, 1), lanes)
    right = (row == column).astype(jnp.float32).astype(jnp.bfloat16)
    spread = lax.dot_general(
        left, right, (((0,), (0,)), ((), ())), preferred_element_type=jnp.float32
    )
    for k, target in enumerate(targets):
        for i in range(2):
            at = (i * count + k) * lanes
            target[i] = spread[:, at : at + lanes]


def gram(vecs, left, wave, colour):
    sites = vecs.shape[2]
    real = vecs[0, colour].astype(jnp.float32)
    imag = vecs[1, colour].astype(jnp.float32)
    cosine = wave[0]
    sine = wave[1]
    phased = jnp.concatenate(
        [
            (cosine * real + sine * imag).astype(jnp.bfloat16),
            (cosine * imag - sine * real).astype(jnp.bfloat16),
        ],
        axis=1,
    )
    return jnp.dot(
        left[:, pl.ds(colour * sites, sites)], phased, preferred_element_type=jnp.float32
    )


def keep(out, total):
    columns = out.shape[-1]
    out[0] = (total[:columns, :columns] + total[columns:, columns:]).astype(out.dtype)
    out[1] = (total[:columns, columns:] - total[columns:, :columns]).astype(out.dtype)


def gram_first(far, near, evecs, momenta, table, trig_in, *rest):
    outs = rest[: len(far)]
    vecs, left, waves, own, trig, moments, units, sems = rest[len(far) :]
    _, colours, sites, columns = vecs.shape
    small = [
        pltpu.make_async_copy(source, target, sems.at[i])
        for i, (source, target) in enumerate(((momenta, moments), (table, units), (trig_in, trig)))
    ]
    large = [pltpu.make_async_copy(evecs, vecs, sems.at[3])]
    for load in small + large:
        load.start()
    for load in small:
        load.wait()
    shifts = far + near
    targets = [own.at[i] for i in range(len(far))] + [waves.at[i] for i in range(len(near))]
    for at in range(0, len(shifts), 4):
        phases(moments, units, trig, shifts[at : at + 4], sites, targets[at : at + 4])
    totals = [None] * len(far)
    for colour in range(colours):
        if colour == 0:
            large[0].wait()
        for part in range(2):
            left[pl.ds(part * columns, columns), pl.ds(colour * sites, sites)] = vecs[part, colour].T
        if len(far) > 4:
            continue
        for i in range(len(far)):
            term = gram(vecs, left, own.at[i], colour)
            totals[i] = term if totals[i] is None else totals[i] + term
    for i, out in enumerate(outs):
        if totals[i] is None:
            totals[i] = sum(gram(vecs, left, own.at[i], colour) for colour in range(colours))
        keep(out, totals[i])


def gram_second(vecs, left, waves, *outs):
    for i, out in enumerate(outs):
        keep(out, sum(gram(vecs, left, waves.at[i], colour) for colour in range(vecs.shape[1])))


def gram_cost(count, vectors):
    _, colours, sites, columns = vectors.shape
    return pl.CostEstimate(
        flops=count * 16 * colours * sites * columns * columns,
        bytes_accessed=4 * colours * sites * columns + count * 4 * columns * columns,
        transcendentals=0,
    )


def partial_elementals(vectors, momenta, table, far, near):
    _, colours, sites, columns = vectors.shape
    angles = np.arange(128, dtype=np.float32) * np.float32(2.0 * math.pi / LS)
    trig = jnp.asarray(np.stack([np.cos(angles), np.sin(angles)] * 4).astype(np.float32))
    shape = (2, columns, columns)
    momenta, table = in_hbm(momenta), in_hbm(table)
    small = [pltpu.SMEM(momenta.shape, jnp.int32), pltpu.SMEM(table.shape, jnp.int32)]
    params = pltpu.CompilerParams(vmem_limit_bytes=LIMIT)
    wave = (2, sites, columns)
    *first, vecs, left, waves = pl.pallas_call(
        functools.partial(gram_first, far, near),
        out_shape=[jax.ShapeDtypeStruct(shape, jnp.bfloat16) for _ in far]
        + [
            jax.ShapeDtypeStruct(vectors.shape, vectors.dtype),
            jax.ShapeDtypeStruct((2 * columns, colours * sites), vectors.dtype),
            jax.ShapeDtypeStruct((len(near),) + wave, jnp.float32),
        ],
        in_specs=[HBM] * 4,
        out_specs=[VMEM] * (len(far) + 3),
        scratch_shapes=[
            pltpu.VMEM((len(far),) + wave, jnp.float32),
            pltpu.VMEM(trig.shape, trig.dtype),
            *small,
            pltpu.SemaphoreType.DMA((4,)),
        ],
        compiler_params=params,
        cost_estimate=gram_cost(len(far), vectors),
        name="gram_far",
    )(in_hbm(vectors), momenta, table, in_hbm(trig))
    second = pl.pallas_call(
        gram_second,
        out_shape=[
            jax.ShapeDtypeStruct(shape, jnp.float32 if k == 0 else jnp.bfloat16) for k in near
        ],
        in_specs=[VMEM] * 3,
        out_specs=[VMEM] * len(near),
        compiler_params=params,
        cost_estimate=gram_cost(len(near), vectors),
        name="gram_near",
    )(vecs, left, waves)
    return dict(zip(far + near, first + list(second)))


def slot_of(masks):
    me = lax.axis_index("tm")
    return me ^ jnp.where(me & 1 == 1, masks[1], masks[0])


def mix_kernel(masks, sink, peramb, table, labels, out, units, times, sems):
    load_units = pltpu.make_async_copy(table, units, sems.at[0])
    load_times = pltpu.make_async_copy(labels, times, sems.at[1])
    load_units.start()
    load_times.start()
    real = sink[0]
    imag = sink[1]
    columns = real.shape[0]
    left = jnp.concatenate(
        [jnp.concatenate([real, -imag], axis=1), jnp.concatenate([imag, real], axis=1)], axis=0
    )
    load_units.wait()
    load_times.wait()
    turns = units[1, lax.axis_index("space")]
    odd = lax.rem(turns, 2)
    phase_real = ((1 - odd) * (1 - turns)).astype(jnp.float32)
    phase_imag = (odd * (2 - turns)).astype(jnp.float32)
    me = lax.axis_index("tm")
    own = times[me]
    for k in range(peramb.shape[0]):
        n = slot_of(masks[k])
        sign = jnp.where(times[n] > own, -1.0, 1.0).astype(jnp.float32)
        right = jnp.concatenate([peramb[n, 0], peramb[n, 1]], axis=0)
        mixed = jnp.dot(left, right, preferred_element_type=jnp.float32)
        mixed_real = mixed[:columns]
        mixed_imag = mixed[columns:]
        turn_real = sign * phase_real
        turn_imag = sign * phase_imag
        out[k, :, pl.ds(0, columns)] = (turn_real * mixed_real - turn_imag * mixed_imag).astype(
            out.dtype
        )
        out[k, :, pl.ds(columns, columns)] = (
            turn_real * mixed_imag + turn_imag * mixed_real
        ).astype(out.dtype)


def mix(sink, peramb, table, labels, masks):
    slots, _, columns, _ = peramb.shape
    return pl.pallas_call(
        functools.partial(mix_kernel, masks),
        out_shape=jax.ShapeDtypeStruct((slots, columns, 2 * columns), jnp.bfloat16),
        in_specs=[VMEM, VMEM, HBM, HBM],
        out_specs=VMEM,
        scratch_shapes=[
            pltpu.SMEM(table.shape, jnp.int32),
            pltpu.SMEM(labels.shape, jnp.int32),
            pltpu.SemaphoreType.DMA((2,)),
        ],
        compiler_params=pltpu.CompilerParams(vmem_limit_bytes=LIMIT),
        cost_estimate=pl.CostEstimate(
            flops=slots * 8 * columns**3, bytes_accessed=slots * 8 * columns**2, transcendentals=0
        ),
        name="mix",
    )(sink, peramb, in_hbm(table), in_hbm(labels))


def close_kernel(ks, masks, before, mixed, *rest):
    sources = rest[: len(ks)]
    out, blocks, sems = rest[len(ks) + before :]
    columns = sources[0].shape[-1]
    stores = []
    for i, (source, k) in enumerate(zip(sources, ks)):
        real = source[0]
        imag = source[1]
        right = jnp.concatenate(
            [jnp.concatenate([real, imag], axis=1), jnp.concatenate([-imag, real], axis=1)], axis=0
        )
        block = lax.dot_general(
            mixed[k], right, (((1,), (1,)), ((), ())), preferred_element_type=jnp.float32
        )
        blocks[i, 0] = block[:, :columns].astype(out.dtype)
        blocks[i, 1] = block[:, columns:].astype(out.dtype)
        store = pltpu.make_async_copy(blocks.at[i], out.at[slot_of(masks[k])], sems.at[i])
        store.start()
        stores.append(store)
    for store in stores:
        store.wait()


def close(mixed, sources, ks, masks, out=None):
    slots, columns, _ = mixed.shape
    before = [] if out is None else [out]
    shape = (slots, 2, columns, columns)
    return pl.pallas_call(
        functools.partial(close_kernel, ks, masks, len(before)),
        out_shape=jax.ShapeDtypeStruct(shape, jnp.bfloat16),
        in_specs=[VMEM] * (1 + len(ks)) + [HBM] * len(before),
        out_specs=HBM,
        scratch_shapes=[
            pltpu.VMEM((len(ks),) + shape[1:], jnp.bfloat16),
            pltpu.SemaphoreType.DMA((len(ks),)),
        ],
        input_output_aliases={1 + len(ks): 0} if before else {},
        compiler_params=pltpu.CompilerParams(vmem_limit_bytes=LIMIT),
        cost_estimate=pl.CostEstimate(
            flops=len(ks) * 8 * columns**3,
            bytes_accessed=len(ks) * 12 * columns**2,
            transcendentals=0,
        ),
        name="close",
    )(mixed, *[sources[k] for k in ks], *before)


def sum_order(space):
    shifts = list(range(1, space))
    return shifts, space // 2


def hop_order(times):
    return [(k, k) for k in range(times - 2, 0, -2)]


def body(space, times, evecs, peramb, momenta, unit_table, time_labels):
    table = unit_table.T
    shifts, far = sum_order(space)
    partials = partial_elementals(evecs[0], momenta, table, shifts[:far], shifts[far:] + [0])
    total = partials[0]
    for shift in shifts:
        pairs = along(space, shift)
        total = total + lax.ppermute(partials[shift], "space", pairs).astype(jnp.float32)
    sink = total.astype(jnp.bfloat16)
    hops = hop_order(times)
    masks = [(0, 0), (1, 1)]
    for even, odd in hops:
        masks += [(even, odd), (odd ^ 1, even ^ 1)]
    sources = {0: sink}
    for i in range(1, len(hops) + 1):
        even, odd = masks[2 * i]
        pairs = [(a, a ^ (odd if a & 1 else even)) for a in range(times)]
        sources[2 * i] = lax.ppermute(sink, "tm", pairs)
    mixed = mix(sink, peramb[0, 0], table, time_labels, masks)
    for i in range(len(hops) + 1):
        pairs = [(a, a ^ 1) for a in range(times)]
        sources[2 * i + 1] = lax.ppermute(sources[2 * i], "tm", pairs)
    out = close(mixed, sources, list(range(times - LATE)), masks)
    return close(mixed, sources, list(range(times - LATE, times)), masks, out)[None, None]


def solution(mesh):
    space, times = mesh.shape["space"], mesh.shape["tm"]
    return jax.shard_map(
        functools.partial(body, space, times),
        mesh=mesh,
        in_specs=(
            P("tm", None, None, "space", None),
            P("tm", "space", None, None, None, None),
            P(),
            P(),
            P(),
        ),
        out_specs=P("tm", "space", None, None, None, None),
        check_vma=False,
    )
```

```python
import functools
import math

import jax
import jax.numpy as jnp
import numpy as np
from jax import lax
from jax.experimental import pallas as pl
from jax.experimental.pallas import tpu as pltpu
from jax.sharding import PartitionSpec as P


LS = 40
LIMIT = 12 * 1024 * 1024
VMEM = pl.BlockSpec(memory_space=pltpu.VMEM)
HBM = pl.BlockSpec(memory_space=pltpu.HBM)


def floor_parts(values, base):
    quotient = jnp.floor((values + 0.5) * (1.0 / base))
    return quotient, values - base * quotient


def in_hbm(value):
    return pltpu.with_memory_space_constraint(value, pltpu.HBM)


def site_parts(count, sites):
    first = (lax.axis_index("space") * sites).astype(jnp.float32)
    site = lax.broadcasted_iota(jnp.int32, (count, sites), 1).astype(jnp.float32) + first
    row, x = floor_parts(site, float(LS))
    if sites * lax.axis_size("space") <= LS * LS:
        return [x, row]
    z, y = floor_parts(row, float(LS))
    return [x, y, z]


def ring(size):
    return [at ^ (at >> 1) for at in range(size)]


def partner(size, shift):
    places = ring(size)
    me = lax.axis_index("space")
    target = jnp.int32(0)
    for at, place in enumerate(places):
        target = jnp.where(me == place, places[(at + shift) % size], target)
    return target


def along(size, shift):
    places = ring(size)
    return [(place, places[(at + shift) % size]) for at, place in enumerate(places)]


def phases(moments, units, trig, shifts, sites, targets):
    count = len(shifts)
    which = lax.broadcasted_iota(jnp.int32, (count, sites), 0)
    rows = [
        units[0, partner(lax.axis_size("space"), shift)]
        for shift in shifts
    ]
    product = jnp.zeros((count, sites), jnp.float32)
    for i, part in enumerate(site_parts(count, sites)):
        factor = jnp.zeros((count, sites), jnp.float32)
        for k, row in enumerate(rows):
            factor = jnp.where(which == k, moments[row, i].astype(jnp.float32), factor)
        product = product + factor * part
    _, turns = floor_parts(product, float(LS))
    index = turns.astype(jnp.int32)
    lanes = trig.shape[1]
    values = []
    for i in range(2):
        table = jnp.broadcast_to(trig[i : i + 1, :], (count, lanes))
        pieces = [
            jnp.take_along_axis(
                table, index[:, at : at + lanes], axis=1, mode="promise_in_bounds"
            )
            for at in range(0, sites, lanes)
        ]
        values.append(jnp.concatenate(pieces, axis=1))
    rest = jnp.concatenate(values, axis=0)
    pieces = []
    for _ in range(3):
        piece = rest.astype(jnp.bfloat16).astype(jnp.float32)
        pieces.append(piece)
        rest = rest - piece
    left = jnp.concatenate(pieces, axis=0).astype(jnp.bfloat16)
    shape = (left.shape[0], 2 * count * lanes)
    row = lax.rem(lax.broadcasted_iota(jnp.int32, shape, 0), 2 * count)
    column = lax.div(lax.broadcasted_iota(jnp.int32, shape, 1), lanes)
    right = (row == column).astype(jnp.float32).astype(jnp.bfloat16)
    spread = lax.dot_general(
        left, right, (((0,), (0,)), ((), ())), preferred_element_type=jnp.float32
    )
    for k, target in enumerate(targets):
        for i in range(2):
            at = (i * count + k) * lanes
            target[i] = spread[:, at : at + lanes]


def gram(vecs, left, wave, colour):
    sites = vecs.shape[2]
    real = vecs[0, colour].astype(jnp.float32)
    imag = vecs[1, colour].astype(jnp.float32)
    cosine = wave[0]
    sine = wave[1]
    phased = jnp.concatenate(
        [
            (cosine * real + sine * imag).astype(jnp.bfloat16),
            (cosine * imag - sine * real).astype(jnp.bfloat16),
        ],
        axis=1,
    )
    return jnp.dot(
        left[:, pl.ds(colour * sites, sites)], phased, preferred_element_type=jnp.float32
    )


def keep(out, total):
    columns = out.shape[-1]
    out[0] = (total[:columns, :columns] + total[columns:, columns:]).astype(out.dtype)
    out[1] = (total[:columns, columns:] - total[columns:, :columns]).astype(out.dtype)


def gram_first(far, near, evecs, momenta, table, trig_in, *rest):
    outs = rest[: len(far)]
    early = rest[len(far) : len(far) + len(near)]
    vecs, left, waves, own, trig, moments, units, sems = rest[len(far) + len(near) :]
    _, colours, sites, columns = vecs.shape
    small = [
        pltpu.make_async_copy(source, target, sems.at[i])
        for i, (source, target) in enumerate(((momenta, moments), (table, units), (trig_in, trig)))
    ]
    large = [pltpu.make_async_copy(evecs, vecs, sems.at[3])]
    for load in small + large:
        load.start()
    for load in small:
        load.wait()
    shifts = far + near
    targets = [own.at[i] for i in range(len(far))] + [waves.at[i] for i in range(len(near))]
    for at in range(0, len(shifts), 4):
        phases(moments, units, trig, shifts[at : at + 4], sites, targets[at : at + 4])
    totals = [None] * len(far)
    for colour in range(colours):
        if colour == 0:
            large[0].wait()
        for part in range(2):
            left[pl.ds(part * columns, columns), pl.ds(colour * sites, sites)] = vecs[part, colour].T
        if len(far) > 4:
            continue
        for i in range(len(far)):
            term = gram(vecs, left, own.at[i], colour)
            totals[i] = term if totals[i] is None else totals[i] + term
    for i, out in enumerate(outs):
        if totals[i] is None:
            totals[i] = sum(gram(vecs, left, own.at[i], colour) for colour in range(colours))
        keep(out, totals[i])

    @pl.when(lax.axis_index("space") == 0)
    def _():
        gram_near(vecs, left, waves, early)


def gram_near(vecs, left, waves, outs):
    for i, out in enumerate(outs):
        keep(out, sum(gram(vecs, left, waves.at[i], colour) for colour in range(vecs.shape[1])))


def gram_second(vecs, left, waves, *rest):
    early = rest[: len(rest) // 2]
    outs = rest[len(rest) // 2 :]

    @pl.when(lax.axis_index("space") == 0)
    def _():
        for out, value in zip(outs, early):
            out[...] = value[...]

    @pl.when(lax.axis_index("space") != 0)
    def _():
        gram_near(vecs, left, waves, outs)


def gram_cost(count, vectors):
    _, colours, sites, columns = vectors.shape
    return pl.CostEstimate(
        flops=count * 16 * colours * sites * columns * columns,
        bytes_accessed=4 * colours * sites * columns + count * 4 * columns * columns,
        transcendentals=0,
    )


def partial_elementals(vectors, momenta, table, far, near):
    _, colours, sites, columns = vectors.shape
    angles = np.arange(128, dtype=np.float32) * np.float32(2.0 * math.pi / LS)
    trig = jnp.asarray(np.stack([np.cos(angles), np.sin(angles)] * 4).astype(np.float32))
    shape = (2, columns, columns)
    momenta, table = in_hbm(momenta), in_hbm(table)
    small = [pltpu.SMEM(momenta.shape, jnp.int32), pltpu.SMEM(table.shape, jnp.int32)]
    params = pltpu.CompilerParams(vmem_limit_bytes=LIMIT)
    wave = (2, sites, columns)
    near_shape = [
        jax.ShapeDtypeStruct(shape, jnp.float32 if k == 0 else jnp.bfloat16) for k in near
    ]
    *first, vecs, left, waves = pl.pallas_call(
        functools.partial(gram_first, far, near),
        out_shape=[jax.ShapeDtypeStruct(shape, jnp.bfloat16) for _ in far]
        + near_shape
        + [
            jax.ShapeDtypeStruct(vectors.shape, vectors.dtype),
            jax.ShapeDtypeStruct((2 * columns, colours * sites), vectors.dtype),
            jax.ShapeDtypeStruct((len(near),) + wave, jnp.float32),
        ],
        in_specs=[HBM] * 4,
        out_specs=[VMEM] * (len(far) + len(near) + 3),
        scratch_shapes=[
            pltpu.VMEM((len(far),) + wave, jnp.float32),
            pltpu.VMEM(trig.shape, trig.dtype),
            *small,
            pltpu.SemaphoreType.DMA((4,)),
        ],
        compiler_params=params,
        cost_estimate=gram_cost(len(far), vectors),
        name="gram_far",
    )(in_hbm(vectors), momenta, table, in_hbm(trig))
    second = pl.pallas_call(
        gram_second,
        out_shape=near_shape,
        in_specs=[VMEM] * (3 + len(near)),
        out_specs=[VMEM] * len(near),
        compiler_params=params,
        cost_estimate=gram_cost(len(near), vectors),
        name="gram_near",
    )(vecs, left, waves, *first[len(far) :])
    return dict(zip(far + near, first[: len(far)] + list(second)))


def slot_of(masks):
    me = lax.axis_index("tm")
    return me ^ jnp.where(me & 1 == 1, masks[1], masks[0])


def mix_kernel(masks, sink, peramb, table, labels, out, units, times, sems):
    load_units = pltpu.make_async_copy(table, units, sems.at[0])
    load_times = pltpu.make_async_copy(labels, times, sems.at[1])
    load_units.start()
    load_times.start()
    real = sink[0]
    imag = sink[1]
    columns = real.shape[0]
    left = jnp.concatenate(
        [jnp.concatenate([real, -imag], axis=1), jnp.concatenate([imag, real], axis=1)], axis=0
    )
    load_units.wait()
    load_times.wait()
    turns = units[1, lax.axis_index("space")]
    odd = lax.rem(turns, 2)
    phase_real = ((1 - odd) * (1 - turns)).astype(jnp.float32)
    phase_imag = (odd * (2 - turns)).astype(jnp.float32)
    me = lax.axis_index("tm")
    own = times[me]
    for k in range(peramb.shape[0]):
        n = slot_of(masks[k])
        sign = jnp.where(times[n] > own, -1.0, 1.0).astype(jnp.float32)
        right = jnp.concatenate([peramb[n, 0], peramb[n, 1]], axis=0)
        mixed = jnp.dot(left, right, preferred_element_type=jnp.float32)
        mixed_real = mixed[:columns]
        mixed_imag = mixed[columns:]
        turn_real = sign * phase_real
        turn_imag = sign * phase_imag
        out[k, :, pl.ds(0, columns)] = (turn_real * mixed_real - turn_imag * mixed_imag).astype(
            out.dtype
        )
        out[k, :, pl.ds(columns, columns)] = (
            turn_real * mixed_imag + turn_imag * mixed_real
        ).astype(out.dtype)


def mix(sink, peramb, table, labels, masks):
    slots, _, columns, _ = peramb.shape
    return pl.pallas_call(
        functools.partial(mix_kernel, masks),
        out_shape=jax.ShapeDtypeStruct((slots, columns, 2 * columns), jnp.bfloat16),
        in_specs=[VMEM, VMEM, HBM, HBM],
        out_specs=VMEM,
        scratch_shapes=[
            pltpu.SMEM(table.shape, jnp.int32),
            pltpu.SMEM(labels.shape, jnp.int32),
            pltpu.SemaphoreType.DMA((2,)),
        ],
        compiler_params=pltpu.CompilerParams(vmem_limit_bytes=LIMIT),
        cost_estimate=pl.CostEstimate(
            flops=slots * 8 * columns**3, bytes_accessed=slots * 8 * columns**2, transcendentals=0
        ),
        name="mix",
    )(sink, peramb, in_hbm(table), in_hbm(labels))


def close_kernel(ks, masks, before, mixed, *rest):
    sources = rest[: len(ks)]
    out, blocks, sems = rest[len(ks) + before :]
    columns = sources[0].shape[-1]
    stores = []
    for i, (source, k) in enumerate(zip(sources, ks)):
        real = source[0]
        imag = source[1]
        right = jnp.concatenate(
            [jnp.concatenate([real, imag], axis=1), jnp.concatenate([-imag, real], axis=1)], axis=0
        )
        block = lax.dot_general(
            mixed[k], right, (((1,), (1,)), ((), ())), preferred_element_type=jnp.float32
        )
        blocks[i, 0] = block[:, :columns].astype(out.dtype)
        blocks[i, 1] = block[:, columns:].astype(out.dtype)
        store = pltpu.make_async_copy(blocks.at[i], out.at[slot_of(masks[k])], sems.at[i])
        store.start()
        stores.append(store)
    for store in stores:
        store.wait()


def close(mixed, sources, ks, masks, out=None):
    slots, columns, _ = mixed.shape
    before = [] if out is None else [out]
    shape = (slots, 2, columns, columns)
    return pl.pallas_call(
        functools.partial(close_kernel, ks, masks, len(before)),
        out_shape=jax.ShapeDtypeStruct(shape, jnp.bfloat16),
        in_specs=[VMEM] * (1 + len(ks)) + [HBM] * len(before),
        out_specs=HBM,
        scratch_shapes=[
            pltpu.VMEM((len(ks),) + shape[1:], jnp.bfloat16),
            pltpu.SemaphoreType.DMA((len(ks),)),
        ],
        input_output_aliases={1 + len(ks): 0} if before else {},
        compiler_params=pltpu.CompilerParams(vmem_limit_bytes=LIMIT),
        cost_estimate=pl.CostEstimate(
            flops=len(ks) * 8 * columns**3,
            bytes_accessed=len(ks) * 12 * columns**2,
            transcendentals=0,
        ),
        name="close",
    )(mixed, *[sources[k] for k in ks], *before)


def sum_order(space):
    shifts = list(range(1, space))
    return shifts, space // 2


def hop_order(times):
    return [(k, k) for k in range(times - 2, 0, -2)]


def body(space, times, evecs, peramb, momenta, unit_table, time_labels):
    table = unit_table.T
    shifts, far = sum_order(space)
    partials = partial_elementals(evecs[0], momenta, table, shifts[:far], shifts[far:] + [0])
    total = partials[0]
    for shift in shifts:
        pairs = along(space, shift)
        total = total + lax.ppermute(partials[shift], "space", pairs).astype(jnp.float32)
    sink = total.astype(jnp.bfloat16)
    hops = hop_order(times)
    masks = [(0, 0), (1, 1)]
    for even, odd in hops:
        masks += [(even, odd), (odd ^ 1, even ^ 1)]
    sources = {0: sink}
    for i in range(1, len(hops) + 1):
        even, odd = masks[2 * i]
        pairs = [(a, a ^ (odd if a & 1 else even)) for a in range(times)]
        sources[2 * i] = lax.ppermute(sink, "tm", pairs)
    mixed = mix(sink, peramb[0, 0], table, time_labels, masks)
    for i in range(len(hops) + 1):
        pairs = [(a, a ^ 1) for a in range(times)]
        sources[2 * i + 1] = lax.ppermute(sources[2 * i], "tm", pairs)
    late = [times - 3, times - 1]
    early = [k for k in range(times) if k not in late]
    out = close(mixed, sources, early, masks)
    return close(mixed, sources, late, masks, out)[None, None]


def solution(mesh):
    space, times = mesh.shape["space"], mesh.shape["tm"]
    return jax.shard_map(
        functools.partial(body, space, times),
        mesh=mesh,
        in_specs=(
            P("tm", None, None, "space", None),
            P("tm", "space", None, None, None, None),
            P(),
            P(),
            P(),
        ),
        out_specs=P("tm", "space", None, None, None, None),
        check_vma=False,
    )
```

```python
import functools
import math

import jax
import jax.numpy as jnp
import numpy as np
from jax import lax
from jax.experimental import pallas as pl
from jax.experimental.pallas import tpu as pltpu
from jax.sharding import PartitionSpec as P


LS = 40
LIMIT = 12 * 1024 * 1024
VMEM = pl.BlockSpec(memory_space=pltpu.VMEM)
HBM = pl.BlockSpec(memory_space=pltpu.HBM)


def floor_parts(values, base):
    quotient = jnp.floor((values + 0.5) * (1.0 / base))
    return quotient, values - base * quotient


def in_hbm(value):
    return pltpu.with_memory_space_constraint(value, pltpu.HBM)


def site_parts(count, sites):
    first = (lax.axis_index("space") * sites).astype(jnp.float32)
    site = lax.broadcasted_iota(jnp.int32, (count, sites), 1).astype(jnp.float32) + first
    row, x = floor_parts(site, float(LS))
    if sites * lax.axis_size("space") <= LS * LS:
        return [x, row]
    z, y = floor_parts(row, float(LS))
    return [x, y, z]


def ring(size):
    return [at ^ (at >> 1) for at in range(size)]


def partner(size, shift):
    places = ring(size)
    me = lax.axis_index("space")
    target = jnp.int32(0)
    for at, place in enumerate(places):
        target = jnp.where(me == place, places[(at + shift) % size], target)
    return target


def along(size, shift):
    places = ring(size)
    return [(place, places[(at + shift) % size]) for at, place in enumerate(places)]


def phases(moments, units, trig, shifts, sites, targets):
    count = len(shifts)
    which = lax.broadcasted_iota(jnp.int32, (count, sites), 0)
    rows = [
        units[0, partner(lax.axis_size("space"), shift)]
        for shift in shifts
    ]
    product = jnp.zeros((count, sites), jnp.float32)
    for i, part in enumerate(site_parts(count, sites)):
        factor = jnp.zeros((count, sites), jnp.float32)
        for k, row in enumerate(rows):
            factor = jnp.where(which == k, moments[row, i].astype(jnp.float32), factor)
        product = product + factor * part
    _, turns = floor_parts(product, float(LS))
    index = turns.astype(jnp.int32)
    lanes = trig.shape[1]
    values = []
    for i in range(2):
        table = jnp.broadcast_to(trig[i : i + 1, :], (count, lanes))
        pieces = [
            jnp.take_along_axis(
                table, index[:, at : at + lanes], axis=1, mode="promise_in_bounds"
            )
            for at in range(0, sites, lanes)
        ]
        values.append(jnp.concatenate(pieces, axis=1))
    rest = jnp.concatenate(values, axis=0)
    pieces = []
    for _ in range(3):
        piece = rest.astype(jnp.bfloat16).astype(jnp.float32)
        pieces.append(piece)
        rest = rest - piece
    left = jnp.concatenate(pieces, axis=0).astype(jnp.bfloat16)
    shape = (left.shape[0], 2 * count * lanes)
    row = lax.rem(lax.broadcasted_iota(jnp.int32, shape, 0), 2 * count)
    column = lax.div(lax.broadcasted_iota(jnp.int32, shape, 1), lanes)
    right = (row == column).astype(jnp.float32).astype(jnp.bfloat16)
    spread = lax.dot_general(
        left, right, (((0,), (0,)), ((), ())), preferred_element_type=jnp.float32
    )
    for k, target in enumerate(targets):
        for i in range(2):
            at = (i * count + k) * lanes
            target[i] = spread[:, at : at + lanes]


def gram(vecs, left, wave, colour):
    sites = vecs.shape[2]
    real = vecs[0, colour].astype(jnp.float32)
    imag = vecs[1, colour].astype(jnp.float32)
    cosine = wave[0]
    sine = wave[1]
    phased = jnp.concatenate(
        [
            (cosine * real + sine * imag).astype(jnp.bfloat16),
            (cosine * imag - sine * real).astype(jnp.bfloat16),
        ],
        axis=1,
    )
    return jnp.dot(
        left[:, pl.ds(colour * sites, sites)], phased, preferred_element_type=jnp.float32
    )


def keep(out, total):
    columns = out.shape[-1]
    out[0] = (total[:columns, :columns] + total[columns:, columns:]).astype(out.dtype)
    out[1] = (total[:columns, columns:] - total[columns:, :columns]).astype(out.dtype)


def gram_first(far, near, evecs, momenta, table, trig_in, *rest):
    outs = rest[: len(far)]
    early = rest[len(far) : len(far) + len(near)]
    vecs, left, waves, own, trig, moments, units, sems = rest[len(far) + len(near) :]
    _, colours, sites, columns = vecs.shape
    small = [
        pltpu.make_async_copy(source, target, sems.at[i])
        for i, (source, target) in enumerate(((momenta, moments), (table, units), (trig_in, trig)))
    ]
    large = [pltpu.make_async_copy(evecs, vecs, sems.at[3])]
    for load in small + large:
        load.start()
    for load in small:
        load.wait()
    shifts = far + near
    targets = [own.at[i] for i in range(len(far))] + [waves.at[i] for i in range(len(near))]
    for at in range(0, len(shifts), 4):
        phases(moments, units, trig, shifts[at : at + 4], sites, targets[at : at + 4])
    totals = [None] * len(far)
    for colour in range(colours):
        if colour == 0:
            large[0].wait()
        for part in range(2):
            left[pl.ds(part * columns, columns), pl.ds(colour * sites, sites)] = vecs[part, colour].T
        if len(far) > 4:
            continue
        for i in range(len(far)):
            term = gram(vecs, left, own.at[i], colour)
            totals[i] = term if totals[i] is None else totals[i] + term
    for i, out in enumerate(outs):
        if totals[i] is None:
            totals[i] = sum(gram(vecs, left, own.at[i], colour) for colour in range(colours))
        keep(out, totals[i])

    @pl.when(lax.axis_index("space") == 0)
    def _():
        gram_near(vecs, left, waves, early)


def gram_near(vecs, left, waves, outs):
    for i, out in enumerate(outs):
        keep(out, sum(gram(vecs, left, waves.at[i], colour) for colour in range(vecs.shape[1])))


def gram_second(vecs, left, waves, *rest):
    early = rest[: len(rest) // 2]
    outs = rest[len(rest) // 2 :]

    @pl.when(lax.axis_index("space") == 0)
    def _():
        for out, value in zip(outs, early):
            out[...] = value[...]

    @pl.when(lax.axis_index("space") != 0)
    def _():
        gram_near(vecs, left, waves, outs)


def gram_cost(count, vectors):
    _, colours, sites, columns = vectors.shape
    return pl.CostEstimate(
        flops=count * 16 * colours * sites * columns * columns,
        bytes_accessed=4 * colours * sites * columns + count * 4 * columns * columns,
        transcendentals=0,
    )


def partial_elementals(vectors, momenta, table, far, near):
    _, colours, sites, columns = vectors.shape
    angles = np.arange(128, dtype=np.float32) * np.float32(2.0 * math.pi / LS)
    trig = jnp.asarray(np.stack([np.cos(angles), np.sin(angles)] * 4).astype(np.float32))
    shape = (2, columns, columns)
    momenta, table = in_hbm(momenta), in_hbm(table)
    small = [pltpu.SMEM(momenta.shape, jnp.int32), pltpu.SMEM(table.shape, jnp.int32)]
    params = pltpu.CompilerParams(vmem_limit_bytes=LIMIT)
    wave = (2, sites, columns)
    near_shape = [
        jax.ShapeDtypeStruct(shape, jnp.float32 if k == 0 else jnp.bfloat16) for k in near
    ]
    *first, vecs, left, waves = pl.pallas_call(
        functools.partial(gram_first, far, near),
        out_shape=[jax.ShapeDtypeStruct(shape, jnp.bfloat16) for _ in far]
        + near_shape
        + [
            jax.ShapeDtypeStruct(vectors.shape, vectors.dtype),
            jax.ShapeDtypeStruct((2 * columns, colours * sites), vectors.dtype),
            jax.ShapeDtypeStruct((len(near),) + wave, jnp.float32),
        ],
        in_specs=[HBM] * 4,
        out_specs=[VMEM] * (len(far) + len(near) + 3),
        scratch_shapes=[
            pltpu.VMEM((len(far),) + wave, jnp.float32),
            pltpu.VMEM(trig.shape, trig.dtype),
            *small,
            pltpu.SemaphoreType.DMA((4,)),
        ],
        compiler_params=params,
        cost_estimate=gram_cost(len(far), vectors),
        name="gram_far",
    )(in_hbm(vectors), momenta, table, in_hbm(trig))
    second = pl.pallas_call(
        gram_second,
        out_shape=near_shape,
        in_specs=[VMEM] * (3 + len(near)),
        out_specs=[VMEM] * len(near),
        compiler_params=params,
        cost_estimate=gram_cost(len(near), vectors),
        name="gram_near",
    )(vecs, left, waves, *first[len(far) :])
    return dict(zip(far + near, first[: len(far)] + list(second)))


def mix_kernel(sink, peramb, table, labels, out, units, times, sems):
    load_units = pltpu.make_async_copy(table, units, sems.at[0])
    load_times = pltpu.make_async_copy(labels, times, sems.at[1])
    load_units.start()
    load_times.start()
    real = sink[0]
    imag = sink[1]
    columns = real.shape[0]
    left = jnp.concatenate(
        [jnp.concatenate([real, -imag], axis=1), jnp.concatenate([imag, real], axis=1)], axis=0
    )
    load_units.wait()
    load_times.wait()
    turns = units[1, lax.axis_index("space")]
    odd = lax.rem(turns, 2)
    phase_real = ((1 - odd) * (1 - turns)).astype(jnp.float32)
    phase_imag = (odd * (2 - turns)).astype(jnp.float32)
    me = lax.axis_index("tm")
    own = times[me]
    for k in range(peramb.shape[0]):
        n = lax.axis_index("tm") ^ k
        sign = jnp.where(times[n] > own, -1.0, 1.0).astype(jnp.float32)
        right = jnp.concatenate([peramb[n, 0], peramb[n, 1]], axis=0)
        mixed = jnp.dot(left, right, preferred_element_type=jnp.float32)
        mixed_real = mixed[:columns]
        mixed_imag = mixed[columns:]
        turn_real = sign * phase_real
        turn_imag = sign * phase_imag
        out[k, :, pl.ds(0, columns)] = (turn_real * mixed_real - turn_imag * mixed_imag).astype(
            out.dtype
        )
        out[k, :, pl.ds(columns, columns)] = (
            turn_real * mixed_imag + turn_imag * mixed_real
        ).astype(out.dtype)


def mix(sink, peramb, table, labels):
    slots, _, columns, _ = peramb.shape
    return pl.pallas_call(
        mix_kernel,
        out_shape=jax.ShapeDtypeStruct((slots, columns, 2 * columns), jnp.bfloat16),
        in_specs=[VMEM, VMEM, HBM, HBM],
        out_specs=VMEM,
        scratch_shapes=[
            pltpu.SMEM(table.shape, jnp.int32),
            pltpu.SMEM(labels.shape, jnp.int32),
            pltpu.SemaphoreType.DMA((2,)),
        ],
        compiler_params=pltpu.CompilerParams(vmem_limit_bytes=LIMIT),
        cost_estimate=pl.CostEstimate(
            flops=slots * 8 * columns**3, bytes_accessed=slots * 8 * columns**2, transcendentals=0
        ),
        name="mix",
    )(sink, peramb, in_hbm(table), in_hbm(labels))


def close_kernel(ks, before, mixed, *rest):
    sources = rest[: len(ks)]
    out, blocks, sems = rest[len(ks) + before :]
    columns = sources[0].shape[-1]
    stores = []
    for i, (source, k) in enumerate(zip(sources, ks)):
        real = source[0]
        imag = source[1]
        right = jnp.concatenate(
            [jnp.concatenate([real, imag], axis=1), jnp.concatenate([-imag, real], axis=1)], axis=0
        )
        block = lax.dot_general(
            mixed[k], right, (((1,), (1,)), ((), ())), preferred_element_type=jnp.float32
        )
        blocks[i, 0] = block[:, :columns].astype(out.dtype)
        blocks[i, 1] = block[:, columns:].astype(out.dtype)
        store = pltpu.make_async_copy(blocks.at[i], out.at[lax.axis_index("tm") ^ k], sems.at[i])
        store.start()
        stores.append(store)
    for store in stores:
        store.wait()


def close(mixed, sources, ks, out=None):
    slots, columns, _ = mixed.shape
    before = [] if out is None else [out]
    shape = (slots, 2, columns, columns)
    return pl.pallas_call(
        functools.partial(close_kernel, ks, len(before)),
        out_shape=jax.ShapeDtypeStruct(shape, jnp.bfloat16),
        in_specs=[VMEM] * (1 + len(ks)) + [HBM] * len(before),
        out_specs=HBM,
        scratch_shapes=[
            pltpu.VMEM((len(ks),) + shape[1:], jnp.bfloat16),
            pltpu.SemaphoreType.DMA((len(ks),)),
        ],
        input_output_aliases={1 + len(ks): 0} if before else {},
        compiler_params=pltpu.CompilerParams(vmem_limit_bytes=LIMIT),
        cost_estimate=pl.CostEstimate(
            flops=len(ks) * 8 * columns**3,
            bytes_accessed=len(ks) * 12 * columns**2,
            transcendentals=0,
        ),
        name="close",
    )(mixed, *[sources[k] for k in ks], *before)


def sum_order(space):
    shifts = list(range(1, space))
    return shifts, space // 2


def hop_order(times):
    return list(range(times - 2, 0, -2)) + [3]


def swap_order(times):
    return [times - 2, 0] + list(range(times - 4, 2, -2))


def body(space, times, evecs, peramb, momenta, unit_table, time_labels):
    table = unit_table.T
    shifts, far = sum_order(space)
    partials = partial_elementals(evecs[0], momenta, table, shifts[:far], shifts[far:] + [0])
    total = partials[0]
    for shift in shifts:
        pairs = along(space, shift)
        total = total + lax.ppermute(partials[shift], "space", pairs).astype(jnp.float32)
    sink = total.astype(jnp.bfloat16)
    hops = hop_order(times)
    sources = {0: sink}
    for k in hops:
        sources[k] = lax.ppermute(sink, "tm", [(a, a ^ k) for a in range(times)])
    mixed = mix(sink, peramb[0, 0], table, time_labels)
    swaps = swap_order(times)
    for k in swaps:
        sources[k ^ 1] = lax.ppermute(sources[k], "tm", [(a, a ^ 1) for a in range(times)])
    late = [k for k in range(times) if k & 1 or k == 2]
    out = close(mixed, sources, [k for k in range(times) if k not in late])
    return close(mixed, sources, late, out)[None, None]


def solution(mesh):
    space, times = mesh.shape["space"], mesh.shape["tm"]
    return jax.shard_map(
        functools.partial(body, space, times),
        mesh=mesh,
        in_specs=(
            P("tm", None, None, "space", None),
            P("tm", "space", None, None, None, None),
            P(),
            P(),
            P(),
        ),
        out_specs=P("tm", "space", None, None, None, None),
        check_vma=False,
    )
```

```python
import functools
import math

import jax
import jax.numpy as jnp
import numpy as np
from jax import lax
from jax.experimental import pallas as pl
from jax.experimental.pallas import tpu as pltpu
from jax.sharding import PartitionSpec as P


LS = 40
LIMIT = 12 * 1024 * 1024
VMEM = pl.BlockSpec(memory_space=pltpu.VMEM)
HBM = pl.BlockSpec(memory_space=pltpu.HBM)


def floor_parts(values, base):
    quotient = jnp.floor((values + 0.5) * (1.0 / base))
    return quotient, values - base * quotient


def in_hbm(value):
    return pltpu.with_memory_space_constraint(value, pltpu.HBM)


def site_parts(count, sites):
    first = (lax.axis_index("space") * sites).astype(jnp.float32)
    site = lax.broadcasted_iota(jnp.int32, (count, sites), 1).astype(jnp.float32) + first
    row, x = floor_parts(site, float(LS))
    if sites * lax.axis_size("space") <= LS * LS:
        return [x, row]
    z, y = floor_parts(row, float(LS))
    return [x, y, z]


def ring(size):
    return [at ^ (at >> 1) for at in range(size)]


def partner(size, shift):
    places = ring(size)
    me = lax.axis_index("space")
    target = jnp.int32(0)
    for at, place in enumerate(places):
        target = jnp.where(me == place, places[(at + shift) % size], target)
    return target


def along(size, shift):
    places = ring(size)
    return [(place, places[(at + shift) % size]) for at, place in enumerate(places)]


def phases(moments, units, trig, shifts, sites, targets):
    count = len(shifts)
    which = lax.broadcasted_iota(jnp.int32, (count, sites), 0)
    rows = [
        units[0, partner(lax.axis_size("space"), shift)]
        for shift in shifts
    ]
    product = jnp.zeros((count, sites), jnp.float32)
    for i, part in enumerate(site_parts(count, sites)):
        factor = jnp.zeros((count, sites), jnp.float32)
        for k, row in enumerate(rows):
            factor = jnp.where(which == k, moments[row, i].astype(jnp.float32), factor)
        product = product + factor * part
    _, turns = floor_parts(product, float(LS))
    index = turns.astype(jnp.int32)
    lanes = trig.shape[1]
    values = []
    for i in range(2):
        table = jnp.broadcast_to(trig[i : i + 1, :], (count, lanes))
        pieces = [
            jnp.take_along_axis(
                table, index[:, at : at + lanes], axis=1, mode="promise_in_bounds"
            )
            for at in range(0, sites, lanes)
        ]
        values.append(jnp.concatenate(pieces, axis=1))
    rest = jnp.concatenate(values, axis=0)
    pieces = []
    for _ in range(3):
        piece = rest.astype(jnp.bfloat16).astype(jnp.float32)
        pieces.append(piece)
        rest = rest - piece
    left = jnp.concatenate(pieces, axis=0).astype(jnp.bfloat16)
    shape = (left.shape[0], 2 * count * lanes)
    row = lax.rem(lax.broadcasted_iota(jnp.int32, shape, 0), 2 * count)
    column = lax.div(lax.broadcasted_iota(jnp.int32, shape, 1), lanes)
    right = (row == column).astype(jnp.float32).astype(jnp.bfloat16)
    spread = lax.dot_general(
        left, right, (((0,), (0,)), ((), ())), preferred_element_type=jnp.float32
    )
    for k, target in enumerate(targets):
        for i in range(2):
            at = (i * count + k) * lanes
            target[i] = spread[:, at : at + lanes]


def gram(vecs, left, wave, colour):
    sites = vecs.shape[2]
    real = vecs[0, colour].astype(jnp.float32)
    imag = vecs[1, colour].astype(jnp.float32)
    cosine = wave[0]
    sine = wave[1]
    phased = jnp.concatenate(
        [
            (cosine * real + sine * imag).astype(jnp.bfloat16),
            (cosine * imag - sine * real).astype(jnp.bfloat16),
        ],
        axis=1,
    )
    return jnp.dot(
        left[:, pl.ds(colour * sites, sites)], phased, preferred_element_type=jnp.float32
    )


def keep(out, total):
    columns = out.shape[-1]
    out[0] = (total[:columns, :columns] + total[columns:, columns:]).astype(out.dtype)
    out[1] = (total[:columns, columns:] - total[columns:, :columns]).astype(out.dtype)


def gram_first(far, near, evecs, momenta, table, trig_in, *rest):
    outs = rest[: len(far)]
    early = rest[len(far) : len(far) + len(near)]
    vecs, left, waves, own, trig, moments, units, sems = rest[len(far) + len(near) :]
    _, colours, sites, columns = vecs.shape
    small = [
        pltpu.make_async_copy(source, target, sems.at[i])
        for i, (source, target) in enumerate(((momenta, moments), (table, units), (trig_in, trig)))
    ]
    large = [pltpu.make_async_copy(evecs, vecs, sems.at[3])]
    for load in small + large:
        load.start()
    for load in small:
        load.wait()
    shifts = far + near
    targets = [own.at[i] for i in range(len(far))] + [waves.at[i] for i in range(len(near))]
    for at in range(0, len(shifts), 4):
        phases(moments, units, trig, shifts[at : at + 4], sites, targets[at : at + 4])
    totals = [None] * len(far)
    for colour in range(colours):
        if colour == 0:
            large[0].wait()
        for part in range(2):
            left[pl.ds(part * columns, columns), pl.ds(colour * sites, sites)] = vecs[part, colour].T
        if len(far) > 4:
            continue
        for i in range(len(far)):
            term = gram(vecs, left, own.at[i], colour)
            totals[i] = term if totals[i] is None else totals[i] + term
    for i, out in enumerate(outs):
        if totals[i] is None:
            totals[i] = sum(gram(vecs, left, own.at[i], colour) for colour in range(colours))
        keep(out, totals[i])

    @pl.when(lax.axis_index("space") == 0)
    def _():
        gram_near(vecs, left, waves, early)


def gram_near(vecs, left, waves, outs):
    for i, out in enumerate(outs):
        keep(out, sum(gram(vecs, left, waves.at[i], colour) for colour in range(vecs.shape[1])))


def gram_second(vecs, left, waves, *rest):
    early = rest[: len(rest) // 2]
    outs = rest[len(rest) // 2 :]

    @pl.when(lax.axis_index("space") == 0)
    def _():
        for out, value in zip(outs, early):
            out[...] = value[...]

    @pl.when(lax.axis_index("space") != 0)
    def _():
        gram_near(vecs, left, waves, outs)


def gram_cost(count, vectors):
    _, colours, sites, columns = vectors.shape
    return pl.CostEstimate(
        flops=count * 16 * colours * sites * columns * columns,
        bytes_accessed=4 * colours * sites * columns + count * 4 * columns * columns,
        transcendentals=0,
    )


def partial_elementals(vectors, momenta, table, far, near):
    _, colours, sites, columns = vectors.shape
    angles = np.arange(128, dtype=np.float32) * np.float32(2.0 * math.pi / LS)
    trig = jnp.asarray(np.stack([np.cos(angles), np.sin(angles)] * 4).astype(np.float32))
    shape = (2, columns, columns)
    momenta, table = in_hbm(momenta), in_hbm(table)
    small = [pltpu.SMEM(momenta.shape, jnp.int32), pltpu.SMEM(table.shape, jnp.int32)]
    params = pltpu.CompilerParams(vmem_limit_bytes=LIMIT)
    wave = (2, sites, columns)
    near_shape = [
        jax.ShapeDtypeStruct(shape, jnp.float32 if k == 0 else jnp.bfloat16) for k in near
    ]
    *first, vecs, left, waves = pl.pallas_call(
        functools.partial(gram_first, far, near),
        out_shape=[jax.ShapeDtypeStruct(shape, jnp.bfloat16) for _ in far]
        + near_shape
        + [
            jax.ShapeDtypeStruct(vectors.shape, vectors.dtype),
            jax.ShapeDtypeStruct((2 * columns, colours * sites), vectors.dtype),
            jax.ShapeDtypeStruct((len(near),) + wave, jnp.float32),
        ],
        in_specs=[HBM] * 4,
        out_specs=[VMEM] * (len(far) + len(near) + 3),
        scratch_shapes=[
            pltpu.VMEM((len(far),) + wave, jnp.float32),
            pltpu.VMEM(trig.shape, trig.dtype),
            *small,
            pltpu.SemaphoreType.DMA((4,)),
        ],
        compiler_params=params,
        cost_estimate=gram_cost(len(far), vectors),
        name="gram_far",
    )(in_hbm(vectors), momenta, table, in_hbm(trig))
    second = pl.pallas_call(
        gram_second,
        out_shape=near_shape,
        in_specs=[VMEM] * (3 + len(near)),
        out_specs=[VMEM] * len(near),
        compiler_params=params,
        cost_estimate=gram_cost(len(near), vectors),
        name="gram_near",
    )(vecs, left, waves, *first[len(far) :])
    return dict(zip(far + near, first[: len(far)] + list(second)))


def turn_kernel(table, labels_in, turns, units, labels, sems):
    loads = [
        pltpu.make_async_copy(source, target, sems.at[i])
        for i, (source, target) in enumerate(((table, units), (labels_in, labels)))
    ]
    for load in loads:
        load.start()
    for load in loads:
        load.wait()
    power = units[1, lax.axis_index("space")]
    odd = lax.rem(power, 2)
    phase_real = ((1 - odd) * (1 - power)).astype(jnp.float32)
    phase_imag = (odd * (2 - power)).astype(jnp.float32)
    me = lax.axis_index("tm")
    own = labels[me]
    for k in range(turns.shape[0]):
        sign = jnp.where(labels[me ^ k] > own, -1.0, 1.0).astype(jnp.float32)
        turns[k, 0] = jnp.full(turns.shape[2:], sign * phase_real, jnp.float32)
        turns[k, 1] = jnp.full(turns.shape[2:], sign * phase_imag, jnp.float32)


def turn_factors(table, labels, columns):
    slots = labels.shape[0]
    return pl.pallas_call(
        turn_kernel,
        out_shape=jax.ShapeDtypeStruct((slots, 2, 8, columns), jnp.float32),
        in_specs=[HBM] * 2,
        out_specs=VMEM,
        scratch_shapes=[
            pltpu.SMEM(table.shape, jnp.int32),
            pltpu.SMEM(labels.shape, jnp.int32),
            pltpu.SemaphoreType.DMA((2,)),
        ],
        compiler_params=pltpu.CompilerParams(vmem_limit_bytes=LIMIT),
        cost_estimate=pl.CostEstimate(
            flops=slots, bytes_accessed=slots * 64 * columns, transcendentals=0
        ),
        name="turn",
    )(in_hbm(table), in_hbm(labels))


def mix_kernel(sink, peramb, turns, out):
    real = sink[0]
    imag = sink[1]
    columns = real.shape[0]
    left = jnp.concatenate(
        [jnp.concatenate([real, -imag], axis=1), jnp.concatenate([imag, real], axis=1)], axis=0
    )
    me = lax.axis_index("tm")
    for k in range(peramb.shape[0]):
        n = me ^ k
        right = jnp.concatenate([peramb[n, 0], peramb[n, 1]], axis=0)
        mixed = jnp.dot(left, right, preferred_element_type=jnp.float32)
        mixed_real = mixed[:columns]
        mixed_imag = mixed[columns:]
        turn_real = turns[k, 0, 0:1, :]
        turn_imag = turns[k, 1, 0:1, :]
        out[k, :, pl.ds(0, columns)] = (turn_real * mixed_real - turn_imag * mixed_imag).astype(
            out.dtype
        )
        out[k, :, pl.ds(columns, columns)] = (
            turn_real * mixed_imag + turn_imag * mixed_real
        ).astype(out.dtype)


def mix(sink, peramb, turns):
    slots, _, columns, _ = peramb.shape
    return pl.pallas_call(
        mix_kernel,
        out_shape=jax.ShapeDtypeStruct((slots, columns, 2 * columns), jnp.bfloat16),
        in_specs=[VMEM] * 3,
        out_specs=VMEM,
        compiler_params=pltpu.CompilerParams(vmem_limit_bytes=LIMIT),
        cost_estimate=pl.CostEstimate(
            flops=slots * 8 * columns**3, bytes_accessed=slots * 8 * columns**2, transcendentals=0
        ),
        name="mix",
    )(sink, peramb, turns)


def close_kernel(ks, before, mixed, *rest):
    sources = rest[: len(ks)]
    out, blocks, sems = rest[len(ks) + before :]
    columns = sources[0].shape[-1]
    stores = []
    for i, (source, k) in enumerate(zip(sources, ks)):
        real = source[0]
        imag = source[1]
        right = jnp.concatenate(
            [jnp.concatenate([real, imag], axis=1), jnp.concatenate([-imag, real], axis=1)], axis=0
        )
        block = lax.dot_general(
            mixed[k], right, (((1,), (1,)), ((), ())), preferred_element_type=jnp.float32
        )
        blocks[i, 0] = block[:, :columns].astype(out.dtype)
        blocks[i, 1] = block[:, columns:].astype(out.dtype)
        store = pltpu.make_async_copy(blocks.at[i], out.at[lax.axis_index("tm") ^ k], sems.at[i])
        store.start()
        stores.append(store)
    for store in stores:
        store.wait()


def close(mixed, sources, ks, out=None):
    slots, columns, _ = mixed.shape
    before = [] if out is None else [out]
    shape = (slots, 2, columns, columns)
    return pl.pallas_call(
        functools.partial(close_kernel, ks, len(before)),
        out_shape=jax.ShapeDtypeStruct(shape, jnp.bfloat16),
        in_specs=[VMEM] * (1 + len(ks)) + [HBM] * len(before),
        out_specs=HBM,
        scratch_shapes=[
            pltpu.VMEM((len(ks),) + shape[1:], jnp.bfloat16),
            pltpu.SemaphoreType.DMA((len(ks),)),
        ],
        input_output_aliases={1 + len(ks): 0} if before else {},
        compiler_params=pltpu.CompilerParams(vmem_limit_bytes=LIMIT),
        cost_estimate=pl.CostEstimate(
            flops=len(ks) * 8 * columns**3,
            bytes_accessed=len(ks) * 12 * columns**2,
            transcendentals=0,
        ),
        name="close",
    )(mixed, *[sources[k] for k in ks], *before)


def sum_order(space):
    shifts = list(range(1, space))
    return shifts, space // 2


def hop_order(times):
    return list(range(times - 2, 0, -2)) + [3]


def swap_order(times):
    return [times - 2, 0] + list(range(times - 4, 2, -2))


def body(space, times, evecs, peramb, momenta, unit_table, time_labels):
    table = unit_table.T
    shifts, far = sum_order(space)
    partials = partial_elementals(evecs[0], momenta, table, shifts[:far], shifts[far:] + [0])
    turns = turn_factors(table, time_labels, peramb.shape[-1])
    total = partials[0]
    for shift in shifts:
        pairs = along(space, shift)
        total = total + lax.ppermute(partials[shift], "space", pairs).astype(jnp.float32)
    sink = total.astype(jnp.bfloat16)
    hops = hop_order(times)
    sources = {0: sink}
    for k in hops:
        sources[k] = lax.ppermute(sink, "tm", [(a, a ^ k) for a in range(times)])
    mixed = mix(sink, peramb[0, 0], turns)
    swaps = swap_order(times)
    for k in swaps:
        sources[k ^ 1] = lax.ppermute(sources[k], "tm", [(a, a ^ 1) for a in range(times)])
    late = [2, 3] + list(range(5, times - 2, 2))
    out = close(mixed, sources, [k for k in range(times) if k not in late])
    return close(mixed, sources, late, out)[None, None]


def solution(mesh):
    space, times = mesh.shape["space"], mesh.shape["tm"]
    return jax.shard_map(
        functools.partial(body, space, times),
        mesh=mesh,
        in_specs=(
            P("tm", None, None, "space", None),
            P("tm", "space", None, None, None, None),
            P(),
            P(),
            P(),
        ),
        out_specs=P("tm", "space", None, None, None, None),
        check_vma=False,
    )
```
